32 devices in a mesh: groups: 2 (over x), mem: 8 (over z, y), tp: 2 (over core).
Axes of the slice: x: 2, y: 2, z: 4, core: 2. Of those that a mesh axis runs over, the one named last changes fastest.
Arguments:
- hidden: bfloat16 [128, 8192], P('groups', 'mem'), parts along dimension 0, may hold values from -6 to 6
- adapter: int32 [128], P('groups'), parts along dimension 0, may hold values from 0 to 31
- page_cache_slot: int32 [256], P('groups'), parts along dimension 0, may hold values from 0 to 127, as said below
- selection: int32 [128, 128], P('groups'), parts along dimension 0, may hold values from 0 to 1, as said below
- query_projection_weight: bfloat16 [8192, 8192], P('mem', 'tp'), may hold values from -0.0625 to 0.0625
- key_projection_weight: bfloat16 [8192, 1024], P('mem', 'tp'), may hold values from -0.0625 to 0.0625
- value_projection_weight: bfloat16 [8192, 1024], P('mem', 'tp'), may hold values from -0.0625 to 0.0625
- adapter_down_weight: bfloat16 [8192, 2048], P('mem'), may hold values from -0.0625 to 0.0625
- adapter_up_weight: bfloat16 [64, 32, 8192], P('mem', None, 'tp'), may hold values from -0.75 to 0.75
- output_projection_weight: bfloat16 [8192, 8192], P('tp', 'mem'), may hold values from -0.0625 to 0.0625
- prefix_key_cache: bfloat16 [256, 128, 1024], P(('groups', 'mem'), None, 'tp'), parts along dimension 0, may hold values from -60 to 60
- prefix_value_cache: bfloat16 [256, 128, 1024], P(('groups', 'mem'), None, 'tp'), parts along dimension 0, may hold values from -6 to 6
Outputs:
- attn_out: bfloat16 [128, 8192], P('groups', 'mem'), parts along dimension 0
The draws below stay inside these ranges and needn't reach their ends.
There are 2 independent parts, one for each index of `groups`. The reference program is written for one: setup_inputs(seed, part) draws one part's arguments, and reference() takes and returns one part's arrays. A program takes and returns all parts, laid end to end along the dimension named above; an argument that names none is the same for every part. Nothing has to cross between parts.
Inputs may be any that keep to these rules, and one draw needn't show every extreme that they name: A permutation: page p is held in cache slot page_cache_slot[p], and slot s lies with index s // 16 of mem. `selection`: every page is selected by 1 to 32 forks; on some index of mem every page held there is selected by exactly 32 forks. A fork may select no page.
All inputs are finite; a program needn't handle non-finite values.
Results may differ from the reference program's by a relative error of at most 0.006.
The reference program's roundings to bfloat16 on the way count: a program that leaves them out, or rounds other values in their place, can miss the bound.
Values may be sent and summed in bfloat16 or wider, within the bound.
A program may use at most 128 MiB of HBM per device.

```python
import math
import jax
import jax.numpy as jnp
import numpy as np
from jax import lax

MODEL_WIDTH = 8192
QUERY_HEADS = 64
KV_HEADS = 8
HEAD_WIDTH = 128
ADAPTER_RANK = 64
ADAPTER_COUNT = 32
PAGE = 128
HOT = 32
PAGE_DEV = 16
FORKS = 64
PAGES = 128


def layout_tables(key):
    base = jax.random.fold_in(key, 4242)
    key_perm, key_count, key_hot, key_rank = jax.random.split(base, 4)
    page_cache_slot = jax.random.permutation(key_perm, PAGES).astype(jnp.int32)
    counts_slot = jax.random.randint(key_count, (PAGES,), 1, HOT + 1)
    devices_count = PAGES // PAGE_DEV
    hot_device = jax.random.randint(key_hot, (), 0, devices_count)
    slot_ids = jnp.arange(PAGES)
    counts_slot = jnp.where(slot_ids // PAGE_DEV == hot_device, HOT, counts_slot)
    counts_page = counts_slot[page_cache_slot]
    fork_orders = jax.vmap(lambda subkey: jax.random.permutation(subkey, FORKS))(jax.random.split(key_rank, PAGES))
    ranking = jnp.argsort(fork_orders, axis=1)
    chosen = (ranking < counts_page[:, None]).astype(jnp.int32)
    return (page_cache_slot, chosen.T)


def draw_page_cache_slot(key, part):
    return layout_tables(key)[0]


def draw_selection(key, part):
    return layout_tables(key)[1]


def draw_prefix_key_cache(key, part):
    key_value = jax.random.fold_in(jax.random.fold_in(key, 77), 1)
    raw = jax.random.normal(key_value, (PAGES, PAGE, KV_HEADS * HEAD_WIDTH))
    return jnp.clip(raw, -6.0, 6.0).astype(jnp.bfloat16)


def with_ends(array, own_key, smallest, high):
    dims = array.shape
    spot = [jax.random.randint(jax.random.fold_in(own_key, axis), (), 0, dims[axis]) for axis in range(len(dims))]
    array = array.at[tuple(spot)].set(smallest)
    longest = dims.index(max(dims))
    spot[longest] = (spot[longest] + 1) % dims[longest]
    return array.at[tuple(spot)].set(high)


def block_scale(rng, shape, pieces, least, high):
    level = 1.0
    for dim, blocks in pieces:
        steps = jax.random.uniform(jax.random.fold_in(jax.random.fold_in(rng, 6), dim), (blocks,), jnp.float32, least / len(pieces), high / len(pieces))
        level = level * jnp.repeat(jnp.exp(steps), shape[dim] // blocks).reshape((-1,) + (1,) * (len(shape) - 1 - dim))
    return level


def rank_table(amount, skew):
    loads = [(1 << 20) // math.isqrt(standing ** skew) + 1 for standing in range(1, amount + 1)]
    scale = 1 + sum(loads) // (1 << 30)
    return np.cumsum(np.array([max(1, weight // scale) for weight in loads]))


def skewed_ids(stream_key, dims, number_of, skew):
    table = rank_table(number_of, skew)
    ticket = jax.random.randint(jax.random.fold_in(stream_key, 1), dims, 0, int(table[number_of - 1]))
    rank = jnp.searchsorted(jnp.asarray(table, jnp.int32), ticket, side="right")
    return jax.random.permutation(jax.random.fold_in(stream_key, 2), number_of)[rank].astype(jnp.int32)


def normal_values(key, extent, width, bound, pieces=(), kind=jnp.bfloat16):
    entries = width * jax.random.normal(key, extent, jnp.float32)
    if pieces:
        entries = entries * block_scale(key, extent, pieces, -0.22, 0.18)
    return jnp.clip(entries, -bound, bound).astype(kind)


def setup_inputs(seed: int = 0, part: int = 0) -> dict:
    key_of = jax.random.split(jax.random.key(seed), 13)
    part_keys = jax.random.split(jax.random.fold_in(key_of[12], part), 13)
    return {
        "hidden": normal_values(part_keys[0], (FORKS, MODEL_WIDTH), 1.0, 6.0, ((1, 8),)),
        "adapter": with_ends(skewed_ids(part_keys[1], (FORKS,), ADAPTER_COUNT, 2), jax.random.fold_in(part_keys[1], 3), 0, ADAPTER_COUNT - 1).astype(jnp.int32),
        "page_cache_slot": draw_page_cache_slot(jax.random.fold_in(jax.random.fold_in(key_of[12], part), 71), part),
        "selection": draw_selection(jax.random.fold_in(jax.random.fold_in(key_of[12], part), 71), part),
        "query_projection_weight": normal_values(key_of[4], (MODEL_WIDTH, QUERY_HEADS * HEAD_WIDTH), MODEL_WIDTH ** -0.5, 0.0625, ((0, 8), (1, 2))),
        "key_projection_weight": normal_values(key_of[5], (MODEL_WIDTH, KV_HEADS * HEAD_WIDTH), MODEL_WIDTH ** -0.5, 0.0625, ((0, 8), (1, 2))),
        "value_projection_weight": normal_values(key_of[6], (MODEL_WIDTH, KV_HEADS * HEAD_WIDTH), MODEL_WIDTH ** -0.5, 0.0625, ((0, 8), (1, 2))),
        "adapter_down_weight": normal_values(key_of[7], (MODEL_WIDTH, ADAPTER_COUNT * ADAPTER_RANK), MODEL_WIDTH ** -0.5, 0.0625, ((0, 8),)),
        "adapter_up_weight": normal_values(key_of[8], (ADAPTER_RANK, ADAPTER_COUNT, QUERY_HEADS * HEAD_WIDTH), ADAPTER_RANK ** -0.5, 0.75, ((0, 8), (2, 2))),
        "output_projection_weight": normal_values(key_of[9], (QUERY_HEADS * HEAD_WIDTH, MODEL_WIDTH), (QUERY_HEADS * HEAD_WIDTH) ** -0.5, 0.0625, ((0, 2), (1, 8))),
        "prefix_key_cache": draw_prefix_key_cache(jax.random.fold_in(jax.random.fold_in(key_of[12], part), 71), part),
        "prefix_value_cache": normal_values(part_keys[11], (PAGES, PAGE, KV_HEADS * HEAD_WIDTH), 1.0, 6.0, ((0, 8), (2, 2))),
    }


adapter_scale = 1.0
neg_floor = -1e30


def reference(hidden, adapter, page_cache_slot, selection, query_projection_weight, key_projection_weight, value_projection_weight, adapter_down_weight, adapter_up_weight, output_projection_weight, prefix_key_cache, prefix_value_cache):
    every_fork_list = hidden.shape[0]
    group_size = QUERY_HEADS // KV_HEADS
    score_scale = HEAD_WIDTH ** -0.5
    onehot = (adapter[:, None] == jnp.arange(ADAPTER_COUNT, dtype=jnp.int32)[None, :]).astype(jnp.float32)
    down_activations = jnp.dot(hidden, adapter_down_weight, preferred_element_type=jnp.float32).reshape(every_fork_list, ADAPTER_COUNT, ADAPTER_RANK)
    rank_acts = jnp.sum(down_activations * onehot[:, None, :].transpose(0, 2, 1), axis=1).astype(jnp.bfloat16)
    spread_factor = (rank_acts.astype(jnp.float32)[:, :, None] * onehot[:, None, :]).astype(jnp.bfloat16)
    spread_factor = spread_factor.reshape(every_fork_list, ADAPTER_RANK * ADAPTER_COUNT)
    adapter_query_delta = jnp.dot(spread_factor, adapter_up_weight.reshape(ADAPTER_RANK * ADAPTER_COUNT, QUERY_HEADS * HEAD_WIDTH), preferred_element_type=jnp.float32)
    query_vectors = (jnp.dot(hidden, query_projection_weight, preferred_element_type=jnp.float32) + adapter_scale * adapter_query_delta).astype(jnp.bfloat16)
    key_new = jnp.dot(hidden, key_projection_weight, preferred_element_type=jnp.float32).astype(jnp.bfloat16)
    value_new = jnp.dot(hidden, value_projection_weight, preferred_element_type=jnp.float32).astype(jnp.bfloat16)
    page_total = page_cache_slot.shape[0]
    page_of_slot = jnp.zeros((page_total,), jnp.int32).at[page_cache_slot].set(jnp.arange(page_total, dtype=jnp.int32))
    query_pad = jnp.concatenate([query_vectors, jnp.zeros((1, QUERY_HEADS * HEAD_WIDTH), jnp.bfloat16)], axis=0)
    query_pad = query_pad.reshape(every_fork_list + 1, KV_HEADS, group_size, HEAD_WIDTH)

    def visit(state_now, scan_items):
        maxima, totals, summed = state_now
        page_keys, page_values, page_id = scan_items
        column = jnp.take(selection, page_id, axis=1)
        chosen = jnp.nonzero(column > 0, size=HOT, fill_value=every_fork_list)[0].astype(jnp.int32)
        picked = query_pad[chosen].astype(jnp.float32)
        keys_f = page_keys.reshape(PAGE, KV_HEADS, HEAD_WIDTH).astype(jnp.float32)
        values_f = page_values.reshape(PAGE, KV_HEADS, HEAD_WIDTH).astype(jnp.float32)
        scores = jnp.einsum('hkgd,tkd->hkgt', picked, keys_f) * score_scale
        page_peak = jnp.max(scores, axis=-1)
        weights = jnp.exp(scores - page_peak[..., None]).astype(jnp.bfloat16).astype(jnp.float32)
        masses = jnp.sum(weights, axis=-1)
        partial_value = jnp.einsum('hkgt,tkd->hkgd', weights, values_f)
        old_max = maxima[chosen]
        new_max = jnp.maximum(old_max, page_peak)
        keep_old = jnp.exp(old_max - new_max)
        fresh_w = jnp.exp(page_peak - new_max)
        totals = totals.at[chosen].set(totals[chosen] * keep_old + masses * fresh_w)
        summed = summed.at[chosen].set(summed[chosen] * keep_old[..., None] + partial_value * fresh_w[..., None])
        maxima = maxima.at[chosen].set(new_max)
        return (maxima, totals, summed), None

    start_state = (jnp.full((every_fork_list + 1, KV_HEADS, group_size), neg_floor, jnp.float32),
                   jnp.zeros((every_fork_list + 1, KV_HEADS, group_size), jnp.float32),
                   jnp.zeros((every_fork_list + 1, KV_HEADS, group_size, HEAD_WIDTH), jnp.float32))
    final_state, unused = lax.scan(visit, start_state, (prefix_key_cache, prefix_value_cache, page_of_slot))
    maxima = final_state[0][:every_fork_list]
    totals = final_state[1][:every_fork_list]
    summed = final_state[2][:every_fork_list]
    query_f = query_vectors.reshape(every_fork_list, KV_HEADS, group_size, HEAD_WIDTH).astype(jnp.float32)
    key_f = key_new.reshape(every_fork_list, KV_HEADS, 1, HEAD_WIDTH).astype(jnp.float32)
    value_f = value_new.reshape(every_fork_list, KV_HEADS, 1, HEAD_WIDTH).astype(jnp.float32)
    own_score = jnp.sum(query_f * key_f, axis=-1) * score_scale
    final_max = jnp.maximum(maxima, own_score)
    old_weight = jnp.exp(maxima - final_max)
    own_weight = jnp.exp(own_score - final_max)
    normalized = (summed * old_weight[..., None] + own_weight[..., None] * value_f) / (totals * old_weight + own_weight)[..., None]
    attended = normalized.astype(jnp.bfloat16).reshape(every_fork_list, QUERY_HEADS * HEAD_WIDTH)
    return jnp.dot(attended, output_projection_weight, preferred_element_type=jnp.float32).astype(jnp.bfloat16)
```

```python
import functools
import math

import jax
import jax.numpy as jnp
from jax import lax
from jax.experimental import pallas as pl
from jax.experimental.pallas import tpu as pltpu
from jax.sharding import PartitionSpec as P

HEAD_WIDTH = 128
ADAPTER_RANK = 64
ADAPTER_COUNT = 32
MESH = pl.DeviceIdType.MESH
F32 = jnp.float32
BF16 = jnp.bfloat16
neg_floor = -1e30
BATCH = 8


def dot(x, y, dims=((1,), (0,))):
    return lax.dot_general(x, y, (dims, ((), ())), preferred_element_type=F32)


def kernel(
    n,
    group_size,
    hidden,
    adapter,
    slots,
    selection,
    wq,
    wk,
    wv,
    down,
    up,
    wo,
    kcache,
    vcache,
    out,
    dbuf,
    kvbuf,
    wqbuf,
    upbuf,
    kbuf,
    vbuf,
    vtbuf,
    wobuf,
    rtx,
    rrx,
    part,
    rx1,
    tx2,
    rx2,
    qfull,
    selx,
    acc,
    turned,
    resa,
    ress,
    rxa,
    rxs,
    txa,
    txs,
    owna,
    owns,
    fxa,
    fxs,
    cfull,
    outp,
    outr,
    loc,
    ssem,
    wsem,
    r1,
    r2,
    gz,
    gy,
    na,
    ns,
    ra,
    rs,
    cz,
    cy,
):
    half = n // 2
    me = lax.axis_index("mem")
    core = lax.axis_index("tp")
    a = me // 2
    b = me % 2
    forks = hidden.shape[0]
    groups = wq.shape[1] // (group_size * HEAD_WIDTH)
    wide = group_size * HEAD_WIDTH
    rows = forks * group_size // n
    lanes = n * rows
    side = half * rows
    mine = b * half + a
    rank_local = up.shape[0]
    pages = kcache.shape[0]
    tokens = kcache.shape[1]
    def send(src, dst, kind, rsem, where):
        copy = pltpu.make_async_remote_copy(
            src_ref=src,
            dst_ref=dst,
            send_sem=ssem.at[kind],
            recv_sem=rsem,
            device_id=where,
            device_id_type=MESH,
        )
        copy.start()

    def take(ref, sem):
        pltpu.make_async_copy(ref, ref, sem).wait()

    def mate():
        return {"mem": me + 1 - 2 * b}

    def far(step):
        return {"mem": 2 * ((a + step) % half) + b}

    order = sorted(range(1, half), key=lambda d: -min(d, half - d))
    spans = sorted(range(1, n), key=lambda o: -min(o, n - o))
    locals_ = []

    def fetch(src, dst):
        copy = pltpu.make_async_copy(src, dst, loc.at[len(locals_)])
        copy.start()
        locals_.append(copy)
        return copy

    dchunks = dbuf.shape[0]
    dwide = dbuf.shape[2]
    get_down = [fetch(down.at[:, pl.ds(c * dwide, dwide)], dbuf.at[c]) for c in range(dchunks)]
    get_k = fetch(wk, kvbuf.at[0])
    get_v = fetch(wv, kvbuf.at[1])
    get_q, get_up = [], []

    def fetch_piece(g):
        columns = pl.ds(g * wide, wide)
        get_q.append(fetch(wq.at[:, columns], wqbuf.at[g]))
        get_up.append(fetch(up.at[:, :, columns], upbuf.at[g]))

    barrier = pltpu.get_barrier_semaphore()
    for o in range(1, n):
        pl.semaphore_signal(barrier, inc=1, device_id={"mem": (me + o) % n}, device_id_type=MESH)
    pl.semaphore_signal(barrier, inc=1, device_id={"tp": 1 - core}, device_id_type=MESH)

    h = hidden[...]
    ids = adapter[...].astype(F32)
    eye = lax.broadcasted_iota(jnp.int32, (forks, forks), 0) == lax.broadcasted_iota(
        jnp.int32, (forks, forks), 1
    )
    id_column = jnp.sum(jnp.where(eye, ids, 0.0), axis=1, keepdims=True)
    per_tile = 128 // ADAPTER_RANK
    lane_part = (
        lax.broadcasted_iota(jnp.int32, (forks, 128), 1) // ADAPTER_RANK
    ).astype(F32)
    folded = jnp.zeros((forks, 128), F32)
    for c in range(dchunks):
        get_down[c].wait()
        if c == 0:
            fetch_piece(0)
        act = dot(h, dbuf[c])
        for t in range(dwide // 128):
            first = (c * (dwide // 128) + t) * per_tile
            folded += jnp.where(
                id_column - float(first) == lane_part, act[:, t * 128 : (t + 1) * 128], 0.0
            )
    for g in range(1, groups):
        fetch_piece(g)
    flipped = jnp.transpose(folded)
    rank_part = flipped[:ADAPTER_RANK]
    for t in range(1, per_tile):
        rank_part += flipped[t * ADAPTER_RANK : (t + 1) * ADAPTER_RANK]
    for j in range(n):
        rtx[j] = rank_part[j * rank_local : (j + 1) * rank_local]
    pl.semaphore_wait(barrier, n)
    for o in spans:
        to = (me + o) % n
        send(rtx.at[to], rrx.at[o - 1], 0, wsem.at[0], {"mem": to})

    def split(g, total):
        for m in range(n):
            first, head = (m // group_size) * rows, (m % group_size) * HEAD_WIDTH
            part[g, m % 2, m // 2] = total[first : first + rows, head : head + HEAD_WIDTH]

    def reduce_near(g):
        send(part.at[g, 1 - b], rx1.at[g], 1, r1.at[g], mate())

    def reduce_far(g):
        take(rx1.at[g], r1.at[g])
        tx2[g] = part[g, b] + rx1[g]
        for d in order:
            send(tx2.at[g, (a + d) % half], rx2.at[g, d - 1], 2, r2.at[g], far(d))

    def reduce_end(g):
        merged = tx2[g, a]
        take(rx2.at[g], r2.at[g])
        for d in order:
            merged = merged + rx2[g, d - 1]
        qfull[g, mine] = merged.astype(BF16)

    def gather(buf, g, kind, zsem, direct):
        own = buf.at[g, mine]
        if direct:
            for o in spans:
                send(own, own, kind, zsem.at[g], {"mem": (me + o) % n})
        else:
            for d in order:
                send(own, own, kind, zsem.at[g], far(d))

    def forward(buf, g, kind, zsem, ysem, direct):
        if not direct:
            take(buf.at[g, pl.ds(0, half - 1)], zsem.at[g])
            block = buf.at[g, pl.ds(b * half, half)]
            send(block, block, kind, ysem.at[g], mate())

    def arrive(buf, g, zsem, ysem, direct):
        if direct:
            take(buf.at[g, pl.ds(0, n - 1)], zsem.at[g])
        else:
            take(buf.at[g, pl.ds(0, half)], ysem.at[g])

    def share(g):
        reduce_end(g)
        gather(qfull, g, 3, gz, DIRECT_Q[g])

    def pass_on(g):
        forward(qfull, g, 3, gz, gy, DIRECT_Q[g])

    def ready(g):
        arrive(qfull, g, gz, gy, DIRECT_Q[g])

    get_k.wait()
    get_v.wait()
    split(groups, jnp.concatenate([dot(h, kvbuf[0]), dot(h, kvbuf[1])], axis=1))
    reduce_near(groups)
    get_vc = fetch(vcache, vbuf)
    get_kc = fetch(kcache, kbuf)
    get_wo = fetch(wo, wobuf)

    lane_id = lax.broadcasted_iota(jnp.int32, (forks, lanes), 1)
    lane_fork = (((lane_id // rows) % half) // (group_size // 2)) * rows + lane_id % rows
    spread_bf = (
        (lane_fork == lax.broadcasted_iota(jnp.int32, (forks, lanes), 0)).astype(F32).astype(BF16)
    )
    slot_ids = me * pages + lax.broadcasted_iota(jnp.int32, (pages, slots.shape[1]), 0)
    match = (slots[...] == slot_ids).astype(F32).astype(BF16)
    chosen = dot(match, selection[...].astype(F32).astype(BF16), ((1,), (1,)))
    selx[...] = dot(chosen.astype(BF16), spread_bf)

    get_q[0].wait()
    base = dot(h, wqbuf[0])
    take(rrx, wsem.at[0])
    ranks = rtx[me]
    for o in range(1, n):
        ranks = ranks + rrx[o - 1]
    ranks = ranks.astype(BF16).astype(F32)
    is_adapter = (
        lax.broadcasted_iota(jnp.int32, (ADAPTER_COUNT, forks), 0) == adapter[...]
    )
    pieces = [jnp.where(is_adapter, ranks[r : r + 1], 0.0) for r in range(rank_local)]
    spread = jnp.transpose(jnp.concatenate(pieces, axis=0)).astype(BF16)

    def produce(g):
        if g:
            get_q[g].wait()
        get_up[g].wait()
        main = dot(h, wqbuf[g]) if g else base
        split(g, main + dot(spread, upbuf[g].reshape(rank_local * ADAPTER_COUNT, wide)))
        reduce_near(g)

    produce(0)
    get_vc.wait()
    vtbuf[:, :, HEAD_WIDTH:, :] = jnp.ones(
        (pages, groups, vtbuf.shape[2] - HEAD_WIDTH, tokens), BF16
    )

    def turn(p, carry):
        for k in range(groups):
            block = vbuf[p, :, k * HEAD_WIDTH : (k + 1) * HEAD_WIDTH]
            vtbuf[p, k, :HEAD_WIDTH, :] = jnp.transpose(block)
        return carry

    batch = math.gcd(pages, BATCH)
    scale = HEAD_WIDTH ** (-0.5)
    scale2 = scale * math.log2(math.e)

    def attend(g):
        columns = pl.ds(g * HEAD_WIDTH, HEAD_WIDTH)
        queries = qfull[g].reshape(lanes, HEAD_WIDTH)
        acc[...] = jnp.zeros_like(acc)
        top0 = jnp.full((1, lanes), neg_floor, F32)
        mass0 = jnp.zeros((1, lanes), F32)

        def block(q, carry):
            top, mass = carry
            first = q * batch
            keys = kbuf[pl.ds(first, batch), :, columns].reshape(batch * tokens, HEAD_WIDTH)
            raw_all = dot(keys, queries, ((1,), (1,)))
            found = []
            new_top = top
            for u in range(batch):
                raw = raw_all[u * tokens : (u + 1) * tokens]
                peak = jnp.max(raw, axis=0, keepdims=True)
                probs = jnp.exp2((raw - peak) * scale2).astype(BF16)
                sums = dot(vtbuf[first + u, g], probs)
                hit = selx[pl.ds(first + u, 1), :] > 0.5
                peak = jnp.where(hit, peak, neg_floor)
                new_top = jnp.maximum(new_top, peak)
                found.append((hit, peak, sums))
            keep = jnp.exp2((top - new_top) * scale2)
            mass = mass * keep
            total = acc[...] * keep
            for hit, peak, sums in found:
                fresh = jnp.where(hit, jnp.exp2((peak - new_top) * scale2), 0.0)
                total = total + sums[:HEAD_WIDTH] * fresh
                mass = mass + sums[HEAD_WIDTH : HEAD_WIDTH + 1] * fresh
            acc[...] = total
            return new_top, mass

        blocks = pages // batch
        return lax.fori_loop(0, blocks, block, (top0, mass0))

    def hand_in(g, top, mass):
        if not DIRECT_R[g]:
            for s in range(2):
                part_lanes = slice(s * side, (s + 1) * side)
                resa[g, s] = acc[:, part_lanes].astype(BF16)
                ress[g, s, 0:1] = top[:, part_lanes]
                ress[g, s, 1:2] = mass[:, part_lanes]
            send(resa.at[g, 1 - b], rxa.at[g], 4, na.at[g], mate())
            send(ress.at[g, 1 - b], rxs.at[g], 5, ns.at[g], mate())
            return
        turned[...] = jnp.transpose(acc[...])
        for s in range(n):
            first = s * rows
            txa[g, s] = turned[first : first + rows].astype(BF16)
            txs[g, s, 0:1] = top[:, first : first + rows]
            txs[g, s, 1:2] = mass[:, first : first + rows]
        for o in spans:
            to = (me + o) % n
            slot = (to % 2) * half + to // 2
            where = {"mem": to}
            send(txa.at[g, slot], fxa.at[g, o - 1], 8, ra.at[g], where)
            send(txs.at[g, slot], fxs.at[g, o - 1], 9, rs.at[g], where)
        owna[g] = turned[pl.ds(pl.multiple_of(mine * rows, rows), rows)]
        owns[g] = txs[g, mine]

    def merge_near(g):
        if DIRECT_R[g]:
            return
        take(rxa.at[g], na.at[g])
        take(rxs.at[g], ns.at[g])
        top_a, top_b = ress[g, b, 0:1], rxs[g, 0:1]
        top = jnp.maximum(top_a, top_b)
        fac_a = jnp.exp2((top_a - top) * scale2)
        fac_b = jnp.exp2((top_b - top) * scale2)
        mass = ress[g, b, 1:2] * fac_a + rxs[g, 1:2] * fac_b
        total = resa[g, b].astype(F32) * fac_a + rxa[g].astype(F32) * fac_b
        turned[:side] = jnp.transpose(total)
        for s in range(half):
            first = s * rows
            txa[g, s] = turned[first : first + rows].astype(BF16)
            txs[g, s, 0:1] = top[:, first : first + rows]
            txs[g, s, 1:2] = mass[:, first : first + rows]
        for d in order:
            slot = (a + d) % half
            send(txa.at[g, slot], fxa.at[g, d - 1], 6, ra.at[g], far(d))
            send(txs.at[g, slot], fxs.at[g, d - 1], 7, rs.at[g], far(d))
        owna[g] = turned[pl.ds(pl.multiple_of(a * rows, rows), rows)]
        owns[g] = txs[g, a]

    def merge(g):
        block = (me // group_size) * (group_size // 2)
        key_new = qfull[groups, (g % 2) * half + block + g // 2].astype(F32)
        at = g + groups
        value_new = qfull[groups, (at % 2) * half + block + at // 2].astype(F32)
        own_score = jnp.sum(qfull[g, mine].astype(F32) * key_new, axis=1, keepdims=True)
        count = n if DIRECT_R[g] else half
        take(fxa.at[g, pl.ds(0, count - 1)], ra.at[g])
        take(fxs.at[g, pl.ds(0, count - 1)], rs.at[g])
        stats = [owns[g, 0:1]] + [fxs[g, o, 0:1] for o in range(count - 1)]
        stats += [owns[g, 1:2]] + [fxs[g, o, 1:2] for o in range(count - 1)]
        columns = jnp.transpose(jnp.concatenate(stats, axis=0))
        tops, masses = columns[:, :count], columns[:, count:]
        top = jnp.maximum(jnp.max(tops, axis=1, keepdims=True), own_score)
        factors = jnp.exp2((tops - top) * scale2)
        own = jnp.exp2((own_score - top) * scale2)
        mass = jnp.sum(masses * factors, axis=1, keepdims=True) + own
        total = owna[g] * factors[:, 0:1] + value_new * own
        for o in range(count - 1):
            total = total + fxa[g, o].astype(F32) * factors[:, o + 1 : o + 2]
        cfull[g, mine] = (total / mass).astype(BF16)
        gather(cfull, g, 10, cz, DIRECT_C[g])

    def pass_context(g):
        forward(cfull, g, 10, cz, cy, DIRECT_C[g])

    wo_ready = []

    def project(g):
        arrive(cfull, g, cz, cy, DIRECT_C[g])
        context = []
        for first in range(0, n, group_size):
            context.append(
                jnp.concatenate(
                    [cfull[g, (m % 2) * half + m // 2] for m in range(first, first + group_size)], axis=1
                )
            )
        context = jnp.concatenate(context, axis=0)
        if not wo_ready:
            get_wo.wait()
            wo_ready.append(True)
        product = dot(context, wobuf[g * wide : (g + 1) * wide, :])
        outp[...] += product


    get_kc.wait()
    outp[...] = jnp.zeros_like(outp)

    def visit(g):
        ready(g)
        hand_in(g, *attend(g))

    steps = {
        "produce": produce,
        "far": reduce_far,
        "turn": lambda g: lax.fori_loop(g * pages // 2, (g + 1) * pages // 2, turn, 0),
        "share": share,
        "pass": pass_on,
        "visit": visit,
        "near": merge_near,
        "ready": ready,
        "merge": merge,
        "context": pass_context,
        "project": project,
    }
    for name, g in order_of(groups):
        steps[name](g)
    send(outp, outr, 11, wsem.at[1], {"tp": 1 - core})
    take(outr, wsem.at[1])
    out[...] = (outp[...] + outr[...]).astype(out.dtype)
    near_r = DIRECT_R.count(False)
    full_r = len(DIRECT_R) - near_r
    sent = [rrx, rx1, rx2, qfull.at[:, pl.ds(0, n - 1)]]
    if near_r:
        first = pl.ds(0, near_r)
        sent += [rxa.at[first], rxs.at[first]]
        sent += [fxa.at[first, pl.ds(0, half - 1)], fxs.at[first, pl.ds(0, half - 1)]]
    else:
        sent += [None] * 4
    if full_r:
        first = pl.ds(0, full_r)
        sent += [fxa.at[first], fxs.at[first]]
    else:
        sent += [None] * 2
    sent += [cfull.at[:, pl.ds(0, n - 1)], outr]
    for kind, ref in enumerate(sent):
        if ref is not None:
            take(ref, ssem.at[kind])


ORDER = (
    ("far", 4),
    ("produce", 1),
    ("produce", 2),
    ("far", 0),
    ("far", 1),
    ("turn", 1),
    ("far", 2),
    ("produce", 3),
    ("share", 1),
    ("share", 0),
    ("share", 2),
    ("far", 3),
    ("share", 4),
    ("pass", 1),
    ("turn", 0),
    ("pass", 0),
    ("pass", 2),
    ("visit", 1),
    ("share", 3),
    ("pass", 3),
    ("visit", 2),
    ("pass", 4),
    ("near", 1),
    ("visit", 0),
    ("near", 2),
    ("visit", 3),
    ("ready", 4),
    ("merge", 1),
    ("near", 0),
    ("near", 3),
    ("context", 1),
    ("merge", 2),
    ("merge", 0),
    ("merge", 3),
    ("context", 3),
    ("context", 2),
    ("context", 0),
    ("project", 1),
    ("project", 2),
    ("project", 3),
    ("project", 0),
)
DIRECT_Q = (False, False, False, True, False)
DIRECT_R = (False, False, False, False)
DIRECT_C = (False, False, False, True)


def order_of(groups):
    if groups == len(DIRECT_R):
        return ORDER
    every = range(groups)
    steps = [("turn", 0), ("turn", 1)] + [("produce", g) for g in range(1, groups)]
    for g in [groups] + list(every):
        steps += [("far", g), ("share", g), ("pass", g)]
    steps += [("ready", groups)]
    for g in every:
        steps += [("visit", g), ("near", g), ("merge", g), ("context", g), ("project", g)]
    return steps


def shards(
    hidden,
    adapter,
    page_cache_slot,
    selection,
    query_projection_weight,
    key_projection_weight,
    value_projection_weight,
    adapter_down_weight,
    adapter_up_weight,
    output_projection_weight,
    prefix_key_cache,
    prefix_value_cache,
):
    n = lax.axis_size("mem")
    half = n // 2
    forks, depth = hidden.shape
    width = query_projection_weight.shape[1]
    kv_width = key_projection_weight.shape[1]
    groups = kv_width // HEAD_WIDTH
    group_size = width // kv_width
    wide = group_size * HEAD_WIDTH
    rows = forks * group_size // n
    lanes = n * rows
    side = half * rows
    out_width = output_projection_weight.shape[1]
    rank_local = adapter_up_weight.shape[0]
    pages, tokens = prefix_key_cache.shape[:2]
    down_width = adapter_down_weight.shape[1]
    chunks = 4
    dma = pltpu.SemaphoreType.DMA
    vmem = pltpu.VMEM
    scratch = [
        vmem((chunks, depth, down_width // chunks), BF16),
        vmem((2, depth, kv_width), BF16),
        vmem((groups, depth, wide), BF16),
        vmem((groups, rank_local, ADAPTER_COUNT, wide), BF16),
        vmem(prefix_key_cache.shape, BF16),
        vmem(prefix_value_cache.shape, BF16),
        vmem((pages, groups, HEAD_WIDTH + 16, tokens), BF16),
        vmem(output_projection_weight.shape, BF16),
        vmem((n, rank_local, forks), F32),
        vmem((n - 1, rank_local, forks), F32),
        vmem((groups + 1, 2, half, rows, HEAD_WIDTH), F32),
        vmem((groups + 1, half, rows, HEAD_WIDTH), F32),
        vmem((groups + 1, half, rows, HEAD_WIDTH), F32),
        vmem((groups + 1, half - 1, rows, HEAD_WIDTH), F32),
        vmem((groups + 1, n, rows, HEAD_WIDTH), BF16),
        vmem((pages, lanes), F32),
        vmem((HEAD_WIDTH, lanes), F32),
        vmem((lanes, HEAD_WIDTH), F32),
        vmem((groups, 2, HEAD_WIDTH, side), BF16),
        vmem((groups, 2, 2, side), F32),
        vmem((groups, HEAD_WIDTH, side), BF16),
        vmem((groups, 2, side), F32),
        vmem((groups, n, rows, HEAD_WIDTH), BF16),
        vmem((groups, n, 2, rows), F32),
        vmem((groups, rows, HEAD_WIDTH), F32),
        vmem((groups, 2, rows), F32),
        vmem((groups, n - 1, rows, HEAD_WIDTH), BF16),
        vmem((groups, n - 1, 2, rows), F32),
        vmem((groups, n, rows, HEAD_WIDTH), BF16),
        vmem((forks, out_width), F32),
        vmem((forks, out_width), F32),
        dma((chunks + 2 + 2 * groups + 3,)),
        dma((12,)),
        dma((2,)),
        dma((groups + 1,)),
        dma((groups + 1,)),
        dma((groups + 1,)),
        dma((groups + 1,)),
        dma((groups,)),
        dma((groups,)),
        dma((groups,)),
        dma((groups,)),
        dma((groups,)),
        dma((groups,)),
    ]
    small = pl.BlockSpec(memory_space=pltpu.VMEM)
    large = pl.BlockSpec(memory_space=pl.ANY)
    return pl.pallas_call(
        functools.partial(kernel, n, group_size),
        out_shape=jax.ShapeDtypeStruct((forks, out_width), BF16),
        in_specs=[small] * 4 + [large] * 8,
        out_specs=small,
        scratch_shapes=scratch,
        compiler_params=pltpu.CompilerParams(
            collective_id=0, has_side_effects=True, vmem_limit_bytes=60 * 1024 * 1024
        ),
    )(
        hidden,
        adapter.reshape(1, forks),
        page_cache_slot.reshape(1, page_cache_slot.shape[0]),
        selection,
        query_projection_weight,
        key_projection_weight,
        value_projection_weight,
        adapter_down_weight,
        adapter_up_weight,
        output_projection_weight,
        prefix_key_cache,
        prefix_value_cache,
    )


def solution(mesh):
    return jax.shard_map(
        shards,
        mesh=mesh,
        in_specs=(
            P("groups", "mem"),
            P("groups"),
            P("groups"),
            P("groups", None),
            P("mem", "tp"),
            P("mem", "tp"),
            P("mem", "tp"),
            P("mem", None),
            P("mem", None, "tp"),
            P("tp", "mem"),
            P(("groups", "mem"), None, "tp"),
            P(("groups", "mem"), None, "tp"),
        ),
        out_specs=P("groups", "mem"),
        check_vma=False,
    )
```

```python
import functools
import math

import jax
import jax.numpy as jnp
from jax import lax
from jax.experimental import pallas as pl
from jax.experimental.pallas import tpu as pltpu
from jax.sharding import PartitionSpec as P

HEAD_WIDTH = 128
ADAPTER_RANK = 64
ADAPTER_COUNT = 32
MESH = pl.DeviceIdType.MESH
F32 = jnp.float32
BF16 = jnp.bfloat16
neg_floor = -1e30
BATCH = 8


def dot(x, y, dims=((1,), (0,))):
    return lax.dot_general(x, y, (dims, ((), ())), preferred_element_type=F32)


def kernel(
    n,
    group_size,
    hidden,
    adapter,
    slots,
    selection,
    wq,
    wk,
    wv,
    down,
    up,
    wo,
    kcache,
    vcache,
    out,
    dbuf,
    kvbuf,
    wqbuf,
    upbuf,
    kbuf,
    vbuf,
    vtbuf,
    wobuf,
    rtx,
    rrx,
    part,
    rx1,
    tx2,
    rx2,
    code1,
    unit1,
    got1,
    gotu1,
    code2,
    unit2,
    got2,
    gotu2,
    qfull,
    selx,
    acc,
    turned,
    resa,
    ress,
    rxa,
    rxs,
    txa,
    txs,
    owna,
    owns,
    fxa,
    fxs,
    cfull,
    outp,
    outr,
    loc,
    ssem,
    wsem,
    r1,
    r2,
    u1,
    u2,
    gz,
    gy,
    na,
    ns,
    ra,
    rs,
    cz,
    cy,
):
    half = n // 2
    me = lax.axis_index("mem")
    core = lax.axis_index("tp")
    a = me // 2
    b = me % 2
    forks = hidden.shape[0]
    groups = wq.shape[1] // (group_size * HEAD_WIDTH)
    wide = group_size * HEAD_WIDTH
    rows = forks * group_size // n
    lanes = n * rows
    side = half * rows
    mine = b * half + a
    rank_local = up.shape[0]
    pages = kcache.shape[0]
    tokens = kcache.shape[1]
    def send(src, dst, kind, rsem, where):
        copy = pltpu.make_async_remote_copy(
            src_ref=src,
            dst_ref=dst,
            send_sem=ssem.at[kind],
            recv_sem=rsem,
            device_id=where,
            device_id_type=MESH,
        )
        copy.start()

    def take(ref, sem):
        pltpu.make_async_copy(ref, ref, sem).wait()

    def mate():
        return {"mem": me + 1 - 2 * b}

    def far(step):
        return {"mem": 2 * ((a + step) % half) + b}

    order = sorted(range(1, half), key=lambda d: -min(d, half - d))
    spans = sorted(range(1, n), key=lambda o: -min(o, n - o))
    locals_ = []

    def fetch(src, dst):
        copy = pltpu.make_async_copy(src, dst, loc.at[len(locals_)])
        copy.start()
        locals_.append(copy)
        return copy

    dchunks = dbuf.shape[0]
    dwide = dbuf.shape[2]
    get_down = [fetch(down.at[:, pl.ds(c * dwide, dwide)], dbuf.at[c]) for c in range(dchunks)]
    get_k = fetch(wk, kvbuf.at[0])
    get_v = fetch(wv, kvbuf.at[1])
    get_q, get_up = [], []

    def fetch_piece(g):
        columns = pl.ds(g * wide, wide)
        get_q.append(fetch(wq.at[:, columns], wqbuf.at[g]))
        get_up.append(fetch(up.at[:, :, columns], upbuf.at[g]))

    barrier = pltpu.get_barrier_semaphore()
    for o in range(1, n):
        pl.semaphore_signal(barrier, inc=1, device_id={"mem": (me + o) % n}, device_id_type=MESH)
    pl.semaphore_signal(barrier, inc=1, device_id={"tp": 1 - core}, device_id_type=MESH)

    h = hidden[...]
    ids = adapter[...].astype(F32)
    eye = lax.broadcasted_iota(jnp.int32, (forks, forks), 0) == lax.broadcasted_iota(
        jnp.int32, (forks, forks), 1
    )
    id_column = jnp.sum(jnp.where(eye, ids, 0.0), axis=1, keepdims=True)
    per_tile = 128 // ADAPTER_RANK
    lane_part = (
        lax.broadcasted_iota(jnp.int32, (forks, 128), 1) // ADAPTER_RANK
    ).astype(F32)
    folded = jnp.zeros((forks, 128), F32)
    for c in range(dchunks):
        get_down[c].wait()
        if c == 0:
            fetch_piece(0)
        act = dot(h, dbuf[c])
        for t in range(dwide // 128):
            first = (c * (dwide // 128) + t) * per_tile
            folded += jnp.where(
                id_column - float(first) == lane_part, act[:, t * 128 : (t + 1) * 128], 0.0
            )
    for g in range(1, groups):
        fetch_piece(g)
    flipped = jnp.transpose(folded)
    rank_part = flipped[:ADAPTER_RANK]
    for t in range(1, per_tile):
        rank_part += flipped[t * ADAPTER_RANK : (t + 1) * ADAPTER_RANK]
    for j in range(n):
        rtx[j] = rank_part[j * rank_local : (j + 1) * rank_local]
    pl.semaphore_wait(barrier, n)
    for o in spans:
        to = (me + o) % n
        send(rtx.at[to], rrx.at[o - 1], 0, wsem.at[0], {"mem": to})

    def split(g, total):
        for m in range(n):
            first, head = (m // group_size) * rows, (m % group_size) * HEAD_WIDTH
            part[g, m % 2, m // 2] = total[first : first + rows, head : head + HEAD_WIDTH]

    def encode(x):
        unit = jnp.maximum(jnp.max(jnp.abs(x), axis=0, keepdims=True), 1e-30) * (1.0 / 32000.0)
        return jnp.round(x * (1.0 / unit)).astype(jnp.int32).astype(jnp.int16), unit

    def decode(code, unit):
        return code.astype(jnp.int32).astype(F32) * unit

    def reduce_near(g):
        if g == groups:
            send(part.at[g, 1 - b], rx1, 1, r1.at[g], mate())
            return
        for s in range(half):
            code1[g, s], unit1[g, s] = encode(part[g, 1 - b, s])
        send(code1.at[g], got1.at[g], 12, r1.at[g], mate())
        send(unit1.at[g], gotu1.at[g], 13, u1.at[g], mate())

    def reduce_far(g):
        if g == groups:
            take(rx1, r1.at[g])
            tx2[g] = part[g, b] + rx1[...]
            for d in order:
                send(tx2.at[g, (a + d) % half], rx2.at[d - 1], 2, r2.at[g], far(d))
            return
        take(got1.at[g], r1.at[g])
        take(gotu1.at[g], u1.at[g])
        for s in range(half):
            total = part[g, b, s] + decode(got1[g, s], gotu1[g, s])
            tx2[g, s] = total
            code2[g, s], unit2[g, s] = encode(total)
        for d in order:
            s = (a + d) % half
            send(code2.at[g, s], got2.at[g, d - 1], 14, r2.at[g], far(d))
            send(unit2.at[g, s], gotu2.at[g, d - 1], 15, u2.at[g], far(d))

    def reduce_end(g):
        merged = tx2[g, a]
        if g == groups:
            take(rx2, r2.at[g])
            for d in order:
                merged = merged + rx2[d - 1]
        else:
            take(got2.at[g], r2.at[g])
            take(gotu2.at[g], u2.at[g])
            for d in order:
                merged = merged + decode(got2[g, d - 1], gotu2[g, d - 1])
        qfull[g, mine] = merged.astype(BF16)

    def gather(buf, g, kind, zsem, direct):
        own = buf.at[g, mine]
        if direct:
            for o in spans:
                send(own, own, kind, zsem.at[g], {"mem": (me + o) % n})
        else:
            for d in order:
                send(own, own, kind, zsem.at[g], far(d))

    def forward(buf, g, kind, zsem, ysem, direct):
        if not direct:
            take(buf.at[g, pl.ds(0, half - 1)], zsem.at[g])
            block = buf.at[g, pl.ds(b * half, half)]
            send(block, block, kind, ysem.at[g], mate())

    def arrive(buf, g, zsem, ysem, direct):
        if direct:
            take(buf.at[g, pl.ds(0, n - 1)], zsem.at[g])
        else:
            take(buf.at[g, pl.ds(0, half)], ysem.at[g])

    def share(g):
        reduce_end(g)
        gather(qfull, g, 3, gz, DIRECT_Q[g])

    def pass_on(g):
        forward(qfull, g, 3, gz, gy, DIRECT_Q[g])

    def ready(g):
        arrive(qfull, g, gz, gy, DIRECT_Q[g])

    get_k.wait()
    get_v.wait()
    split(groups, jnp.concatenate([dot(h, kvbuf[0]), dot(h, kvbuf[1])], axis=1))
    reduce_near(groups)
    get_vc = fetch(vcache, vbuf)
    get_kc = fetch(kcache, kbuf)
    get_wo = fetch(wo, wobuf)

    lane_id = lax.broadcasted_iota(jnp.int32, (forks, lanes), 1)
    lane_fork = (((lane_id // rows) % half) // (group_size // 2)) * rows + lane_id % rows
    spread_bf = (
        (lane_fork == lax.broadcasted_iota(jnp.int32, (forks, lanes), 0)).astype(F32).astype(BF16)
    )
    slot_ids = me * pages + lax.broadcasted_iota(jnp.int32, (pages, slots.shape[1]), 0)
    match = (slots[...] == slot_ids).astype(F32).astype(BF16)
    chosen = dot(match, selection[...].astype(F32).astype(BF16), ((1,), (1,)))
    selx[...] = dot(chosen.astype(BF16), spread_bf)

    get_q[0].wait()
    base = dot(h, wqbuf[0])
    take(rrx, wsem.at[0])
    ranks = rtx[me]
    for o in range(1, n):
        ranks = ranks + rrx[o - 1]
    ranks = ranks.astype(BF16).astype(F32)
    is_adapter = (
        lax.broadcasted_iota(jnp.int32, (ADAPTER_COUNT, forks), 0) == adapter[...]
    )
    pieces = [jnp.where(is_adapter, ranks[r : r + 1], 0.0) for r in range(rank_local)]
    spread = jnp.transpose(jnp.concatenate(pieces, axis=0)).astype(BF16)

    def produce(g):
        if g:
            get_q[g].wait()
        get_up[g].wait()
        main = dot(h, wqbuf[g]) if g else base
        split(g, main + dot(spread, upbuf[g].reshape(rank_local * ADAPTER_COUNT, wide)))
        reduce_near(g)

    produce(0)
    get_vc.wait()
    vtbuf[:, :, HEAD_WIDTH:, :] = jnp.ones(
        (pages, groups, vtbuf.shape[2] - HEAD_WIDTH, tokens), BF16
    )

    def turn(p, carry):
        for k in range(groups):
            block = vbuf[p, :, k * HEAD_WIDTH : (k + 1) * HEAD_WIDTH]
            vtbuf[p, k, :HEAD_WIDTH, :] = jnp.transpose(block)
        return carry

    batch = math.gcd(pages, BATCH)
    scale = HEAD_WIDTH ** (-0.5)
    scale2 = scale * math.log2(math.e)

    def attend(g):
        columns = pl.ds(g * HEAD_WIDTH, HEAD_WIDTH)
        queries = qfull[g].reshape(lanes, HEAD_WIDTH)
        acc[...] = jnp.zeros_like(acc)
        top0 = jnp.full((1, lanes), neg_floor, F32)
        mass0 = jnp.zeros((1, lanes), F32)

        def block(q, carry):
            top, mass = carry
            first = q * batch
            keys = kbuf[pl.ds(first, batch), :, columns].reshape(batch * tokens, HEAD_WIDTH)
            raw_all = dot(keys, queries, ((1,), (1,)))
            found = []
            new_top = top
            for u in range(batch):
                raw = raw_all[u * tokens : (u + 1) * tokens]
                peak = jnp.max(raw, axis=0, keepdims=True)
                probs = jnp.exp2((raw - peak) * scale2).astype(BF16)
                sums = dot(vtbuf[first + u, g], probs)
                hit = selx[pl.ds(first + u, 1), :] > 0.5
                peak = jnp.where(hit, peak, neg_floor)
                new_top = jnp.maximum(new_top, peak)
                found.append((hit, peak, sums))
            keep = jnp.exp2((top - new_top) * scale2)
            mass = mass * keep
            total = acc[...] * keep
            for hit, peak, sums in found:
                fresh = jnp.where(hit, jnp.exp2((peak - new_top) * scale2), 0.0)
                total = total + sums[:HEAD_WIDTH] * fresh
                mass = mass + sums[HEAD_WIDTH : HEAD_WIDTH + 1] * fresh
            acc[...] = total
            return new_top, mass

        blocks = pages // batch
        return lax.fori_loop(0, blocks, block, (top0, mass0))

    def hand_in(g, top, mass):
        if not DIRECT_R[g]:
            for s in range(2):
                part_lanes = slice(s * side, (s + 1) * side)
                resa[g, s] = acc[:, part_lanes].astype(BF16)
                ress[g, s, 0:1] = top[:, part_lanes]
                ress[g, s, 1:2] = mass[:, part_lanes]
            send(resa.at[g, 1 - b], rxa.at[g], 4, na.at[g], mate())
            send(ress.at[g, 1 - b], rxs.at[g], 5, ns.at[g], mate())
            return
        turned[...] = jnp.transpose(acc[...])
        for s in range(n):
            first = s * rows
            txa[g, s] = turned[first : first + rows].astype(BF16)
            txs[g, s, 0:1] = top[:, first : first + rows]
            txs[g, s, 1:2] = mass[:, first : first + rows]
        for o in spans:
            to = (me + o) % n
            slot = (to % 2) * half + to // 2
            where = {"mem": to}
            send(txa.at[g, slot], fxa.at[g, o - 1], 8, ra.at[g], where)
            send(txs.at[g, slot], fxs.at[g, o - 1], 9, rs.at[g], where)
        owna[g] = turned[pl.ds(pl.multiple_of(mine * rows, rows), rows)]
        owns[g] = txs[g, mine]

    def merge_near(g):
        if DIRECT_R[g]:
            return
        take(rxa.at[g], na.at[g])
        take(rxs.at[g], ns.at[g])
        top_a, top_b = ress[g, b, 0:1], rxs[g, 0:1]
        top = jnp.maximum(top_a, top_b)
        fac_a = jnp.exp2((top_a - top) * scale2)
        fac_b = jnp.exp2((top_b - top) * scale2)
        mass = ress[g, b, 1:2] * fac_a + rxs[g, 1:2] * fac_b
        total = resa[g, b].astype(F32) * fac_a + rxa[g].astype(F32) * fac_b
        turned[:side] = jnp.transpose(total)
        for s in range(half):
            first = s * rows
            txa[g, s] = turned[first : first + rows].astype(BF16)
            txs[g, s, 0:1] = top[:, first : first + rows]
            txs[g, s, 1:2] = mass[:, first : first + rows]
        for d in order:
            slot = (a + d) % half
            send(txa.at[g, slot], fxa.at[g, d - 1], 6, ra.at[g], far(d))
            send(txs.at[g, slot], fxs.at[g, d - 1], 7, rs.at[g], far(d))
        owna[g] = turned[pl.ds(pl.multiple_of(a * rows, rows), rows)]
        owns[g] = txs[g, a]

    def merge(g):
        block = (me // group_size) * (group_size // 2)
        key_new = qfull[groups, (g % 2) * half + block + g // 2].astype(F32)
        at = g + groups
        value_new = qfull[groups, (at % 2) * half + block + at // 2].astype(F32)
        own_score = jnp.sum(qfull[g, mine].astype(F32) * key_new, axis=1, keepdims=True)
        count = n if DIRECT_R[g] else half
        take(fxa.at[g, pl.ds(0, count - 1)], ra.at[g])
        take(fxs.at[g, pl.ds(0, count - 1)], rs.at[g])
        stats = [owns[g, 0:1]] + [fxs[g, o, 0:1] for o in range(count - 1)]
        stats += [owns[g, 1:2]] + [fxs[g, o, 1:2] for o in range(count - 1)]
        columns = jnp.transpose(jnp.concatenate(stats, axis=0))
        tops, masses = columns[:, :count], columns[:, count:]
        top = jnp.maximum(jnp.max(tops, axis=1, keepdims=True), own_score)
        factors = jnp.exp2((tops - top) * scale2)
        own = jnp.exp2((own_score - top) * scale2)
        mass = jnp.sum(masses * factors, axis=1, keepdims=True) + own
        total = owna[g] * factors[:, 0:1] + value_new * own
        for o in range(count - 1):
            total = total + fxa[g, o].astype(F32) * factors[:, o + 1 : o + 2]
        cfull[g, mine] = (total / mass).astype(BF16)
        gather(cfull, g, 10, cz, DIRECT_C[g])

    def pass_context(g):
        forward(cfull, g, 10, cz, cy, DIRECT_C[g])

    wo_ready = []

    def project(g):
        arrive(cfull, g, cz, cy, DIRECT_C[g])
        context = []
        for first in range(0, n, group_size):
            context.append(
                jnp.concatenate(
                    [cfull[g, (m % 2) * half + m // 2] for m in range(first, first + group_size)], axis=1
                )
            )
        context = jnp.concatenate(context, axis=0)
        if not wo_ready:
            get_wo.wait()
            wo_ready.append(True)
        product = dot(context, wobuf[g * wide : (g + 1) * wide, :])
        outp[...] += product


    get_kc.wait()
    outp[...] = jnp.zeros_like(outp)

    def visit(g):
        ready(g)
        hand_in(g, *attend(g))

    steps = {
        "produce": produce,
        "far": reduce_far,
        "turn": lambda g: lax.fori_loop(g * pages // 2, (g + 1) * pages // 2, turn, 0),
        "share": share,
        "pass": pass_on,
        "visit": visit,
        "near": merge_near,
        "ready": ready,
        "merge": merge,
        "context": pass_context,
        "project": project,
    }
    for name, g in order_of(groups):
        steps[name](g)
    send(outp, outr, 11, wsem.at[1], {"tp": 1 - core})
    take(outr, wsem.at[1])
    out[...] = (outp[...] + outr[...]).astype(out.dtype)
    near_r = DIRECT_R.count(False)
    full_r = len(DIRECT_R) - near_r
    sent = [rrx, rx1, rx2, qfull.at[:, pl.ds(0, n - 1)]]
    if near_r:
        first = pl.ds(0, near_r)
        sent += [rxa.at[first], rxs.at[first]]
        sent += [fxa.at[first, pl.ds(0, half - 1)], fxs.at[first, pl.ds(0, half - 1)]]
    else:
        sent += [None] * 4
    if full_r:
        first = pl.ds(0, full_r)
        sent += [fxa.at[first], fxs.at[first]]
    else:
        sent += [None] * 2
    sent += [cfull.at[:, pl.ds(0, n - 1)], outr, got1, gotu1, got2, gotu2]
    for kind, ref in enumerate(sent):
        if ref is not None:
            take(ref, ssem.at[kind])


ORDER = (
    ("far", 4),
    ("produce", 1),
    ("produce", 2),
    ("far", 0),
    ("produce", 3),
    ("turn", 0),
    ("far", 1),
    ("far", 2),
    ("share", 0),
    ("share", 1),
    ("far", 3),
    ("share", 2),
    ("turn", 1),
    ("pass", 0),
    ("share", 4),
    ("pass", 1),
    ("share", 3),
    ("visit", 0),
    ("pass", 2),
    ("visit", 1),
    ("near", 0),
    ("pass", 4),
    ("visit", 2),
    ("pass", 3),
    ("near", 1),
    ("visit", 3),
    ("ready", 4),
    ("merge", 0),
    ("near", 2),
    ("near", 3),
    ("merge", 1),
    ("context", 0),
    ("merge", 2),
    ("merge", 3),
    ("context", 1),
    ("context", 2),
    ("project", 1),
    ("context", 3),
    ("project", 0),
    ("project", 3),
    ("project", 2),
)
DIRECT_Q = (False, False, True, True, False)
DIRECT_R = (False, False, False, False)
DIRECT_C = (False, False, False, True)


def order_of(groups):
    if groups == len(DIRECT_R):
        return ORDER
    every = range(groups)
    steps = [("turn", 0), ("turn", 1)] + [("produce", g) for g in range(1, groups)]
    for g in [groups] + list(every):
        steps += [("far", g), ("share", g), ("pass", g)]
    steps += [("ready", groups)]
    for g in every:
        steps += [("visit", g), ("near", g), ("merge", g), ("context", g), ("project", g)]
    return steps


def shards(
    hidden,
    adapter,
    page_cache_slot,
    selection,
    query_projection_weight,
    key_projection_weight,
    value_projection_weight,
    adapter_down_weight,
    adapter_up_weight,
    output_projection_weight,
    prefix_key_cache,
    prefix_value_cache,
):
    n = lax.axis_size("mem")
    half = n // 2
    forks, depth = hidden.shape
    width = query_projection_weight.shape[1]
    kv_width = key_projection_weight.shape[1]
    groups = kv_width // HEAD_WIDTH
    group_size = width // kv_width
    wide = group_size * HEAD_WIDTH
    rows = forks * group_size // n
    lanes = n * rows
    side = half * rows
    out_width = output_projection_weight.shape[1]
    rank_local = adapter_up_weight.shape[0]
    pages, tokens = prefix_key_cache.shape[:2]
    down_width = adapter_down_weight.shape[1]
    chunks = 4
    dma = pltpu.SemaphoreType.DMA
    vmem = pltpu.VMEM
    scratch = [
        vmem((chunks, depth, down_width // chunks), BF16),
        vmem((2, depth, kv_width), BF16),
        vmem((groups, depth, wide), BF16),
        vmem((groups, rank_local, ADAPTER_COUNT, wide), BF16),
        vmem(prefix_key_cache.shape, BF16),
        vmem(prefix_value_cache.shape, BF16),
        vmem((pages, groups, HEAD_WIDTH + 16, tokens), BF16),
        vmem(output_projection_weight.shape, BF16),
        vmem((n, rank_local, forks), F32),
        vmem((n - 1, rank_local, forks), F32),
        vmem((groups + 1, 2, half, rows, HEAD_WIDTH), F32),
        vmem((half, rows, HEAD_WIDTH), F32),
        vmem((groups + 1, half, rows, HEAD_WIDTH), F32),
        vmem((half - 1, rows, HEAD_WIDTH), F32),
        vmem((groups, half, rows, HEAD_WIDTH), jnp.int16),
        vmem((groups, half, 1, HEAD_WIDTH), F32),
        vmem((groups, half, rows, HEAD_WIDTH), jnp.int16),
        vmem((groups, half, 1, HEAD_WIDTH), F32),
        vmem((groups, half, rows, HEAD_WIDTH), jnp.int16),
        vmem((groups, half, 1, HEAD_WIDTH), F32),
        vmem((groups, half - 1, rows, HEAD_WIDTH), jnp.int16),
        vmem((groups, half - 1, 1, HEAD_WIDTH), F32),
        vmem((groups + 1, n, rows, HEAD_WIDTH), BF16),
        vmem((pages, lanes), F32),
        vmem((HEAD_WIDTH, lanes), F32),
        vmem((lanes, HEAD_WIDTH), F32),
        vmem((groups, 2, HEAD_WIDTH, side), BF16),
        vmem((groups, 2, 2, side), F32),
        vmem((groups, HEAD_WIDTH, side), BF16),
        vmem((groups, 2, side), F32),
        vmem((groups, n, rows, HEAD_WIDTH), BF16),
        vmem((groups, n, 2, rows), F32),
        vmem((groups, rows, HEAD_WIDTH), F32),
        vmem((groups, 2, rows), F32),
        vmem((groups, n - 1, rows, HEAD_WIDTH), BF16),
        vmem((groups, n - 1, 2, rows), F32),
        vmem((groups, n, rows, HEAD_WIDTH), BF16),
        vmem((forks, out_width), F32),
        vmem((forks, out_width), F32),
        dma((chunks + 2 + 2 * groups + 3,)),
        dma((16,)),
        dma((2,)),
        dma((groups + 1,)),
        dma((groups + 1,)),
        dma((groups,)),
        dma((groups,)),
        dma((groups + 1,)),
        dma((groups + 1,)),
        dma((groups,)),
        dma((groups,)),
        dma((groups,)),
        dma((groups,)),
        dma((groups,)),
        dma((groups,)),
    ]
    small = pl.BlockSpec(memory_space=pltpu.VMEM)
    large = pl.BlockSpec(memory_space=pl.ANY)
    return pl.pallas_call(
        functools.partial(kernel, n, group_size),
        out_shape=jax.ShapeDtypeStruct((forks, out_width), BF16),
        in_specs=[small] * 4 + [large] * 8,
        out_specs=small,
        scratch_shapes=scratch,
        compiler_params=pltpu.CompilerParams(
            collective_id=0, has_side_effects=True, vmem_limit_bytes=60 * 1024 * 1024
        ),
    )(
        hidden,
        adapter.reshape(1, forks),
        page_cache_slot.reshape(1, page_cache_slot.shape[0]),
        selection,
        query_projection_weight,
        key_projection_weight,
        value_projection_weight,
        adapter_down_weight,
        adapter_up_weight,
        output_projection_weight,
        prefix_key_cache,
        prefix_value_cache,
    )


def solution(mesh):
    return jax.shard_map(
        shards,
        mesh=mesh,
        in_specs=(
            P("groups", "mem"),
            P("groups"),
            P("groups"),
            P("groups", None),
            P("mem", "tp"),
            P("mem", "tp"),
            P("mem", "tp"),
            P("mem", None),
            P("mem", None, "tp"),
            P("tp", "mem"),
            P(("groups", "mem"), None, "tp"),
            P(("groups", "mem"), None, "tp"),
        ),
        out_specs=P("groups", "mem"),
        check_vma=False,
    )
```

```python
import functools
import math

import jax
import jax.numpy as jnp
from jax import lax
from jax.experimental import pallas as pl
from jax.experimental.pallas import tpu as pltpu
from jax.sharding import PartitionSpec as P

HEAD_WIDTH = 128
ADAPTER_RANK = 64
ADAPTER_COUNT = 32
MESH = pl.DeviceIdType.MESH
F32 = jnp.float32
BF16 = jnp.bfloat16
neg_floor = -1e30
BATCH = 8


def dot(x, y, dims=((1,), (0,))):
    return lax.dot_general(x, y, (dims, ((), ())), preferred_element_type=F32)


def kernel(
    n,
    group_size,
    hidden_in,
    adapter_in,
    slots_in,
    selection_in,
    wq,
    wk,
    wv,
    down,
    up,
    wo,
    kcache,
    vcache,
    total_a,
    total_b,
    hidden,
    adapter,
    slots,
    selection,
    dbuf,
    kvbuf,
    wqbuf,
    upbuf,
    kbuf,
    vbuf,
    vtbuf,
    wobuf,
    rtx,
    rrx,
    part,
    tx2,
    code1,
    unit1,
    got1,
    gotu1,
    code2,
    unit2,
    got2,
    gotu2,
    qfull,
    selx,
    acc,
    turned,
    resa,
    ress,
    rxa,
    rxs,
    txa,
    txs,
    owna,
    owns,
    fxa,
    fxs,
    cfull,
    outp,
    loc,
    ssem,
    wsem,
    r1,
    r2,
    u1,
    u2,
    gz,
    gy,
    na,
    ns,
    ra,
    rs,
    cz,
    cy,
):
    half = n // 2
    me = lax.axis_index("mem")
    core = lax.axis_index("tp")
    a = me // 2
    b = me % 2
    forks = hidden.shape[0]
    groups = wq.shape[1] // (group_size * HEAD_WIDTH)
    wide = group_size * HEAD_WIDTH
    rows = forks * group_size // n
    lanes = n * rows
    side = half * rows
    mine = b * half + a
    rank_local = up.shape[0]
    pages = kcache.shape[0]
    tokens = kcache.shape[1]
    def send(src, dst, kind, rsem, where):
        copy = pltpu.make_async_remote_copy(
            src_ref=src,
            dst_ref=dst,
            send_sem=ssem.at[kind],
            recv_sem=rsem,
            device_id=where,
            device_id_type=MESH,
        )
        copy.start()

    def take(ref, sem):
        pltpu.make_async_copy(ref, ref, sem).wait()

    def mate():
        return {"mem": me + 1 - 2 * b}

    def far(step):
        return {"mem": 2 * ((a + step) % half) + b}

    order = sorted(range(1, half), key=lambda d: -min(d, half - d))
    spans = sorted(range(1, n), key=lambda o: -min(o, n - o))
    locals_ = []

    def fetch(src, dst):
        copy = pltpu.make_async_copy(src, dst, loc.at[len(locals_)])
        copy.start()
        locals_.append(copy)
        return copy

    dchunks = dbuf.shape[0]
    dwide = dbuf.shape[2]
    get_small = [
        fetch(hidden_in, hidden),
        fetch(adapter_in, adapter),
    ]
    get_down = [fetch(down.at[:, pl.ds(c * dwide, dwide)], dbuf.at[c]) for c in range(dchunks)]
    get_q, get_up = [], []

    def fetch_piece(g):
        columns = pl.ds(g * wide, wide)
        get_q.append(fetch(wq.at[:, columns], wqbuf.at[g]))
        get_up.append(fetch(up.at[:, :, columns], upbuf.at[g]))

    barrier = pltpu.get_barrier_semaphore()
    for o in range(1, n):
        pl.semaphore_signal(barrier, inc=1, device_id={"mem": (me + o) % n}, device_id_type=MESH)
    pl.semaphore_signal(barrier, inc=1, device_id={"tp": 1 - core}, device_id_type=MESH)

    for item in get_small:
        item.wait()
    h = hidden[...]
    ids = adapter[...].astype(F32)
    eye = lax.broadcasted_iota(jnp.int32, (forks, forks), 0) == lax.broadcasted_iota(
        jnp.int32, (forks, forks), 1
    )
    id_column = jnp.sum(jnp.where(eye, ids, 0.0), axis=1, keepdims=True)
    per_tile = 128 // ADAPTER_RANK
    lane_part = (
        lax.broadcasted_iota(jnp.int32, (forks, 128), 1) // ADAPTER_RANK
    ).astype(F32)
    folded = jnp.zeros((forks, 128), F32)
    for c in range(dchunks):
        get_down[c].wait()
        if c == dchunks - 2:
            get_k = fetch(wk, kvbuf.at[0])
            get_v = fetch(wv, kvbuf.at[1])
            fetch_piece(0)
            get_slots = fetch(slots_in, slots)
            get_selection = fetch(selection_in, selection)
        act = dot(h, dbuf[c])
        for t in range(dwide // 128):
            first = (c * (dwide // 128) + t) * per_tile
            folded += jnp.where(
                id_column - float(first) == lane_part, act[:, t * 128 : (t + 1) * 128], 0.0
            )
    for g in range(1, groups):
        fetch_piece(g)
    flipped = jnp.transpose(folded)
    rank_part = flipped[:ADAPTER_RANK]
    for t in range(1, per_tile):
        rank_part += flipped[t * ADAPTER_RANK : (t + 1) * ADAPTER_RANK]
    for j in range(n):
        rtx[j] = rank_part[j * rank_local : (j + 1) * rank_local]
    pl.semaphore_wait(barrier, n)
    for o in spans:
        to = (me + o) % n
        send(rtx.at[to], rrx.at[o - 1], 0, wsem.at[0], {"mem": to})

    def split(g, total):
        for m in range(n):
            first, head = (m // group_size) * rows, (m % group_size) * HEAD_WIDTH
            part[g, m % 2, m // 2] = total[first : first + rows, head : head + HEAD_WIDTH]

    def encode(x):
        unit = jnp.maximum(jnp.max(jnp.abs(x), axis=0, keepdims=True), 1e-30) * (1.0 / 32000.0)
        return jnp.round(x * (1.0 / unit)).astype(jnp.int32).astype(jnp.int16), unit

    def decode(code, unit):
        return code.astype(jnp.int32).astype(F32) * unit

    def reduce_near(g):
        for s in range(half):
            code1[g, s], unit1[g, s] = encode(part[g, 1 - b, s])
        send(code1.at[g], got1.at[g], 1, r1.at[g], mate())
        send(unit1.at[g], gotu1.at[g], 12, u1.at[g], mate())

    def reduce_far(g):
        take(got1.at[g], r1.at[g])
        take(gotu1.at[g], u1.at[g])
        for s in range(half):
            total = part[g, b, s] + decode(got1[g, s], gotu1[g, s])
            tx2[g, s] = total
            code2[g, s], unit2[g, s] = encode(total)
        for d in order:
            s = (a + d) % half
            send(code2.at[g, s], got2.at[g, d - 1], 2, r2.at[g], far(d))
            send(unit2.at[g, s], gotu2.at[g, d - 1], 13, u2.at[g], far(d))

    def reduce_end(g):
        merged = tx2[g, a]
        take(got2.at[g], r2.at[g])
        take(gotu2.at[g], u2.at[g])
        for d in order:
            merged = merged + decode(got2[g, d - 1], gotu2[g, d - 1])
        qfull[g, mine] = merged.astype(BF16)

    def gather(buf, g, kind, zsem, direct):
        own = buf.at[g, mine]
        if direct:
            for o in spans:
                send(own, own, kind, zsem.at[g], {"mem": (me + o) % n})
        else:
            for d in order:
                send(own, own, kind, zsem.at[g], far(d))

    def forward(buf, g, kind, zsem, ysem, direct):
        if not direct:
            take(buf.at[g, pl.ds(0, half - 1)], zsem.at[g])
            block = buf.at[g, pl.ds(b * half, half)]
            send(block, block, kind, ysem.at[g], mate())

    def arrive(buf, g, zsem, ysem, direct):
        if direct:
            take(buf.at[g, pl.ds(0, n - 1)], zsem.at[g])
        else:
            take(buf.at[g, pl.ds(0, half)], ysem.at[g])

    def share(g):
        reduce_end(g)
        gather(qfull, g, 3, gz, DIRECT_Q[g])

    def pass_on(g):
        forward(qfull, g, 3, gz, gy, DIRECT_Q[g])

    def ready(g):
        arrive(qfull, g, gz, gy, DIRECT_Q[g])

    get_k.wait()
    get_v.wait()
    split(groups, jnp.concatenate([dot(h, kvbuf[0]), dot(h, kvbuf[1])], axis=1))
    reduce_near(groups)
    get_vc = fetch(vcache, vbuf)
    get_kc = fetch(kcache, kbuf)
    get_wo = fetch(wo, wobuf)

    get_slots.wait()
    get_selection.wait()
    lane_id = lax.broadcasted_iota(jnp.int32, (forks, lanes), 1)
    lane_fork = (((lane_id // rows) % half) // (group_size // 2)) * rows + lane_id % rows
    spread_bf = (
        (lane_fork == lax.broadcasted_iota(jnp.int32, (forks, lanes), 0)).astype(F32).astype(BF16)
    )
    slot_ids = me * pages + lax.broadcasted_iota(jnp.int32, (pages, slots.shape[1]), 0)
    match = (slots[...] == slot_ids).astype(F32).astype(BF16)
    chosen = dot(match, selection[...].astype(F32).astype(BF16), ((1,), (1,)))
    selx[...] = dot(chosen.astype(BF16), spread_bf)

    get_q[0].wait()
    base = dot(h, wqbuf[0])
    take(rrx, wsem.at[0])
    ranks = rtx[me]
    for o in range(1, n):
        ranks = ranks + rrx[o - 1]
    ranks = ranks.astype(BF16).astype(F32)
    is_adapter = (
        lax.broadcasted_iota(jnp.int32, (ADAPTER_COUNT, forks), 0) == adapter[...]
    )
    pieces = [jnp.where(is_adapter, ranks[r : r + 1], 0.0) for r in range(rank_local)]
    spread = jnp.transpose(jnp.concatenate(pieces, axis=0)).astype(BF16)

    def produce(g):
        if g:
            get_q[g].wait()
        get_up[g].wait()
        main = dot(h, wqbuf[g]) if g else base
        split(g, main + dot(spread, upbuf[g].reshape(rank_local * ADAPTER_COUNT, wide)))
        reduce_near(g)

    produce(0)
    get_vc.wait()
    vtbuf[:, :, HEAD_WIDTH:, :] = jnp.ones(
        (pages, groups, vtbuf.shape[2] - HEAD_WIDTH, tokens), BF16
    )

    def turn(p, carry):
        for k in range(groups):
            block = vbuf[p, :, k * HEAD_WIDTH : (k + 1) * HEAD_WIDTH]
            vtbuf[p, k, :HEAD_WIDTH, :] = jnp.transpose(block)
        return carry

    batch = math.gcd(pages, BATCH)
    scale = HEAD_WIDTH ** (-0.5)
    scale2 = scale * math.log2(math.e)

    def attend(g):
        columns = pl.ds(g * HEAD_WIDTH, HEAD_WIDTH)
        queries = qfull[g].reshape(lanes, HEAD_WIDTH)
        acc[...] = jnp.zeros_like(acc)
        top0 = jnp.full((1, lanes), neg_floor, F32)
        mass0 = jnp.zeros((1, lanes), F32)

        def block(q, carry):
            top, mass = carry
            first = q * batch
            keys = kbuf[pl.ds(first, batch), :, columns].reshape(batch * tokens, HEAD_WIDTH)
            raw_all = dot(keys, queries, ((1,), (1,)))
            found = []
            new_top = top
            for u in range(batch):
                raw = raw_all[u * tokens : (u + 1) * tokens]
                peak = jnp.max(raw, axis=0, keepdims=True)
                probs = jnp.exp2((raw - peak) * scale2).astype(BF16)
                sums = dot(vtbuf[first + u, g], probs)
                hit = selx[pl.ds(first + u, 1), :] > 0.5
                peak = jnp.where(hit, peak, neg_floor)
                new_top = jnp.maximum(new_top, peak)
                found.append((hit, peak, sums))
            keep = jnp.exp2((top - new_top) * scale2)
            mass = mass * keep
            total = acc[...] * keep
            for hit, peak, sums in found:
                fresh = jnp.where(hit, jnp.exp2((peak - new_top) * scale2), 0.0)
                total = total + sums[:HEAD_WIDTH] * fresh
                mass = mass + sums[HEAD_WIDTH : HEAD_WIDTH + 1] * fresh
            acc[...] = total
            return new_top, mass

        blocks = pages // batch
        return lax.fori_loop(0, blocks, block, (top0, mass0))

    def hand_in(g, top, mass):
        if not DIRECT_R[g]:
            for s in range(2):
                part_lanes = slice(s * side, (s + 1) * side)
                resa[g, s] = acc[:, part_lanes].astype(BF16)
                ress[g, s, 0:1] = top[:, part_lanes]
                ress[g, s, 1:2] = mass[:, part_lanes]
            send(resa.at[g, 1 - b], rxa.at[g], 4, na.at[g], mate())
            send(ress.at[g, 1 - b], rxs.at[g], 5, ns.at[g], mate())
            return
        turned[...] = jnp.transpose(acc[...])
        for s in range(n):
            first = s * rows
            txa[g, s] = turned[first : first + rows].astype(BF16)
            txs[g, s, 0:1] = top[:, first : first + rows]
            txs[g, s, 1:2] = mass[:, first : first + rows]
        for o in spans:
            to = (me + o) % n
            slot = (to % 2) * half + to // 2
            where = {"mem": to}
            send(txa.at[g, slot], fxa.at[g, o - 1], 8, ra.at[g], where)
            send(txs.at[g, slot], fxs.at[g, o - 1], 9, rs.at[g], where)
        owna[g] = turned[pl.ds(pl.multiple_of(mine * rows, rows), rows)]
        owns[g] = txs[g, mine]

    def merge_near(g):
        if DIRECT_R[g]:
            return
        take(rxa.at[g], na.at[g])
        take(rxs.at[g], ns.at[g])
        top_a, top_b = ress[g, b, 0:1], rxs[g, 0:1]
        top = jnp.maximum(top_a, top_b)
        fac_a = jnp.exp2((top_a - top) * scale2)
        fac_b = jnp.exp2((top_b - top) * scale2)
        mass = ress[g, b, 1:2] * fac_a + rxs[g, 1:2] * fac_b
        total = resa[g, b].astype(F32) * fac_a + rxa[g].astype(F32) * fac_b
        turned[:side] = jnp.transpose(total)
        for s in range(half):
            first = s * rows
            txa[g, s] = turned[first : first + rows].astype(BF16)
            txs[g, s, 0:1] = top[:, first : first + rows]
            txs[g, s, 1:2] = mass[:, first : first + rows]
        for d in order:
            slot = (a + d) % half
            send(txa.at[g, slot], fxa.at[g, d - 1], 6, ra.at[g], far(d))
            send(txs.at[g, slot], fxs.at[g, d - 1], 7, rs.at[g], far(d))
        owna[g] = turned[pl.ds(pl.multiple_of(a * rows, rows), rows)]
        owns[g] = txs[g, a]

    def merge(g):
        block = (me // group_size) * (group_size // 2)
        key_new = qfull[groups, (g % 2) * half + block + g // 2].astype(F32)
        at = g + groups
        value_new = qfull[groups, (at % 2) * half + block + at // 2].astype(F32)
        own_score = jnp.sum(qfull[g, mine].astype(F32) * key_new, axis=1, keepdims=True)
        count = n if DIRECT_R[g] else half
        take(fxa.at[g, pl.ds(0, count - 1)], ra.at[g])
        take(fxs.at[g, pl.ds(0, count - 1)], rs.at[g])
        stats = [owns[g, 0:1]] + [fxs[g, o, 0:1] for o in range(count - 1)]
        stats += [owns[g, 1:2]] + [fxs[g, o, 1:2] for o in range(count - 1)]
        columns = jnp.transpose(jnp.concatenate(stats, axis=0))
        tops, masses = columns[:, :count], columns[:, count:]
        top = jnp.maximum(jnp.max(tops, axis=1, keepdims=True), own_score)
        factors = jnp.exp2((tops - top) * scale2)
        own = jnp.exp2((own_score - top) * scale2)
        mass = jnp.sum(masses * factors, axis=1, keepdims=True) + own
        total = owna[g] * factors[:, 0:1] + value_new * own
        for o in range(count - 1):
            total = total + fxa[g, o].astype(F32) * factors[:, o + 1 : o + 2]
        cfull[g, mine] = (total / mass).astype(BF16)
        gather(cfull, g, 10, cz, DIRECT_C[g])

    def pass_context(g):
        forward(cfull, g, 10, cz, cy, DIRECT_C[g])

    wo_ready = []

    def project(g):
        arrive(cfull, g, cz, cy, DIRECT_C[g])
        context = []
        for first in range(0, n, group_size):
            context.append(
                jnp.concatenate(
                    [cfull[g, (m % 2) * half + m // 2] for m in range(first, first + group_size)], axis=1
                )
            )
        context = jnp.concatenate(context, axis=0)
        if not wo_ready:
            get_wo.wait()
            wo_ready.append(True)
        product = dot(context, wobuf[g * wide : (g + 1) * wide, :])
        outp[...] += product


    get_kc.wait()
    outp[...] = jnp.zeros_like(outp)

    def visit(g):
        ready(g)
        hand_in(g, *attend(g))

    steps = {
        "produce": produce,
        "far": reduce_far,
        "turn": lambda g: lax.fori_loop(g * pages // 2, (g + 1) * pages // 2, turn, 0),
        "share": share,
        "pass": pass_on,
        "visit": visit,
        "near": merge_near,
        "ready": ready,
        "merge": merge,
        "context": pass_context,
        "project": project,
    }
    for name, g in order_of(groups):
        steps[name](g)
    keep = fetch(outp, total_a)
    send(outp, total_b, 11, wsem.at[1], {"tp": 1 - core})
    take(total_b, wsem.at[1])
    keep.wait()
    near_r = DIRECT_R.count(False)
    full_r = len(DIRECT_R) - near_r
    sent = [rrx, got1, got2, qfull.at[:, pl.ds(0, n - 1)]]
    if near_r:
        first = pl.ds(0, near_r)
        sent += [rxa.at[first], rxs.at[first]]
        sent += [fxa.at[first, pl.ds(0, half - 1)], fxs.at[first, pl.ds(0, half - 1)]]
    else:
        sent += [None] * 4
    if full_r:
        first = pl.ds(0, full_r)
        sent += [fxa.at[first], fxs.at[first]]
    else:
        sent += [None] * 2
    sent += [cfull.at[:, pl.ds(0, n - 1)], total_b, gotu1, gotu2]
    for kind, ref in enumerate(sent):
        if ref is not None:
            take(ref, ssem.at[kind])


ORDER = (
    ("produce", 1),
    ("produce", 2),
    ("far", 4),
    ("far", 0),
    ("far", 1),
    ("produce", 3),
    ("turn", 1),
    ("far", 2),
    ("share", 0),
    ("share", 1),
    ("far", 3),
    ("share", 2),
    ("turn", 0),
    ("pass", 2),
    ("pass", 0),
    ("pass", 1),
    ("share", 4),
    ("share", 3),
    ("visit", 0),
    ("visit", 1),
    ("visit", 2),
    ("pass", 3),
    ("near", 0),
    ("pass", 4),
    ("near", 1),
    ("visit", 3),
    ("near", 2),
    ("ready", 4),
    ("merge", 0),
    ("near", 3),
    ("merge", 1),
    ("context", 0),
    ("merge", 2),
    ("merge", 3),
    ("context", 1),
    ("context", 2),
    ("project", 1),
    ("context", 3),
    ("project", 0),
    ("project", 3),
    ("project", 2),
)
DIRECT_Q = (False, False, True, True, False)
DIRECT_R = (False, False, False, False)
DIRECT_C = (False, False, False, True)


def order_of(groups):
    if groups == len(DIRECT_R):
        return ORDER
    every = range(groups)
    steps = [("turn", 0), ("turn", 1)] + [("produce", g) for g in range(1, groups)]
    for g in [groups] + list(every):
        steps += [("far", g), ("share", g), ("pass", g)]
    steps += [("ready", groups)]
    for g in every:
        steps += [("visit", g), ("near", g), ("merge", g), ("context", g), ("project", g)]
    return steps


def shards(
    hidden,
    adapter,
    page_cache_slot,
    selection,
    query_projection_weight,
    key_projection_weight,
    value_projection_weight,
    adapter_down_weight,
    adapter_up_weight,
    output_projection_weight,
    prefix_key_cache,
    prefix_value_cache,
):
    n = lax.axis_size("mem")
    half = n // 2
    forks, depth = hidden.shape
    width = query_projection_weight.shape[1]
    kv_width = key_projection_weight.shape[1]
    groups = kv_width // HEAD_WIDTH
    group_size = width // kv_width
    wide = group_size * HEAD_WIDTH
    rows = forks * group_size // n
    lanes = n * rows
    side = half * rows
    out_width = output_projection_weight.shape[1]
    rank_local = adapter_up_weight.shape[0]
    pages, tokens = prefix_key_cache.shape[:2]
    down_width = adapter_down_weight.shape[1]
    chunks = 4
    dma = pltpu.SemaphoreType.DMA
    vmem = pltpu.VMEM
    scratch = [
        vmem((forks, depth), BF16),
        vmem((1, forks), jnp.int32),
        vmem((1, page_cache_slot.shape[0]), jnp.int32),
        vmem(selection.shape, jnp.int32),
        vmem((chunks, depth, down_width // chunks), BF16),
        vmem((2, depth, kv_width), BF16),
        vmem((groups, depth, wide), BF16),
        vmem((groups, rank_local, ADAPTER_COUNT, wide), BF16),
        vmem(prefix_key_cache.shape, BF16),
        vmem(prefix_value_cache.shape, BF16),
        vmem((pages, groups, HEAD_WIDTH + 16, tokens), BF16),
        vmem(output_projection_weight.shape, BF16),
        vmem((n, rank_local, forks), F32),
        vmem((n - 1, rank_local, forks), F32),
        vmem((groups + 1, 2, half, rows, HEAD_WIDTH), F32),
        vmem((groups + 1, half, rows, HEAD_WIDTH), F32),
        vmem((groups + 1, half, rows, HEAD_WIDTH), jnp.int16),
        vmem((groups + 1, half, 1, HEAD_WIDTH), F32),
        vmem((groups + 1, half, rows, HEAD_WIDTH), jnp.int16),
        vmem((groups + 1, half, 1, HEAD_WIDTH), F32),
        vmem((groups + 1, half, rows, HEAD_WIDTH), jnp.int16),
        vmem((groups + 1, half, 1, HEAD_WIDTH), F32),
        vmem((groups + 1, half - 1, rows, HEAD_WIDTH), jnp.int16),
        vmem((groups + 1, half - 1, 1, HEAD_WIDTH), F32),
        vmem((groups + 1, n, rows, HEAD_WIDTH), BF16),
        vmem((pages, lanes), F32),
        vmem((HEAD_WIDTH, lanes), F32),
        vmem((lanes, HEAD_WIDTH), F32),
        vmem((groups, 2, HEAD_WIDTH, side), BF16),
        vmem((groups, 2, 2, side), F32),
        vmem((groups, HEAD_WIDTH, side), BF16),
        vmem((groups, 2, side), F32),
        vmem((groups, n, rows, HEAD_WIDTH), BF16),
        vmem((groups, n, 2, rows), F32),
        vmem((groups, rows, HEAD_WIDTH), F32),
        vmem((groups, 2, rows), F32),
        vmem((groups, n - 1, rows, HEAD_WIDTH), BF16),
        vmem((groups, n - 1, 2, rows), F32),
        vmem((groups, n, rows, HEAD_WIDTH), BF16),
        vmem((forks, out_width), F32),
        dma((chunks + 2 + 2 * groups + 8,)),
        dma((14,)),
        dma((2,)),
        dma((groups + 1,)),
        dma((groups + 1,)),
        dma((groups + 1,)),
        dma((groups + 1,)),
        dma((groups + 1,)),
        dma((groups + 1,)),
        dma((groups,)),
        dma((groups,)),
        dma((groups,)),
        dma((groups,)),
        dma((groups,)),
        dma((groups,)),
    ]
    large = pl.BlockSpec(memory_space=pl.ANY)
    halves = pl.pallas_call(
        functools.partial(kernel, n, group_size),
        out_shape=[jax.ShapeDtypeStruct((forks, out_width), F32)] * 2,
        in_specs=[large] * 12,
        out_specs=[large] * 2,
        scratch_shapes=scratch,
        compiler_params=pltpu.CompilerParams(
            collective_id=0, has_side_effects=True, vmem_limit_bytes=60 * 1024 * 1024
        ),
    )(
        hidden,
        adapter.reshape(1, forks),
        page_cache_slot.reshape(1, page_cache_slot.shape[0]),
        selection,
        query_projection_weight,
        key_projection_weight,
        value_projection_weight,
        adapter_down_weight,
        adapter_up_weight,
        output_projection_weight,
        prefix_key_cache,
        prefix_value_cache,
    )
    return (halves[0] + halves[1]).astype(BF16)


def solution(mesh):
    return jax.shard_map(
        shards,
        mesh=mesh,
        in_specs=(
            P("groups", "mem"),
            P("groups"),
            P("groups"),
            P("groups", None),
            P("mem", "tp"),
            P("mem", "tp"),
            P("mem", "tp"),
            P("mem", None),
            P("mem", None, "tp"),
            P("tp", "mem"),
            P(("groups", "mem"), None, "tp"),
            P(("groups", "mem"), None, "tp"),
        ),
        out_specs=P("groups", "mem"),
        check_vma=False,
    )
```

```python
import functools
import math

import jax
import jax.numpy as jnp
from jax import lax
from jax.experimental import pallas as pl
from jax.experimental.pallas import tpu as pltpu
from jax.sharding import PartitionSpec as P

HEAD_WIDTH = 128
ADAPTER_RANK = 64
ADAPTER_COUNT = 32
MESH = pl.DeviceIdType.MESH
F32 = jnp.float32
BF16 = jnp.bfloat16
neg_floor = -1e30
BATCH = 8


def dot(x, y, dims=((1,), (0,))):
    return lax.dot_general(x, y, (dims, ((), ())), preferred_element_type=F32)


def kernel(
    n,
    group_size,
    hidden_in,
    adapter_in,
    slots_in,
    selection_in,
    wq,
    wk,
    wv,
    down,
    up,
    wo,
    kcache,
    vcache,
    total_a,
    total_b,
    hidden,
    adapter,
    slots,
    selection,
    dbuf,
    kvbuf,
    wqbuf,
    upbuf,
    kbuf,
    vbuf,
    vtbuf,
    wobuf,
    rtx,
    rrx,
    part,
    tx2,
    code0,
    unit0,
    code1,
    unit1,
    got1,
    gotu1,
    code2,
    unit2,
    got2,
    gotu2,
    qfull,
    selx,
    acc,
    turned,
    resa,
    ress,
    rxa,
    rxs,
    txa,
    txs,
    owna,
    owns,
    fxa,
    fxs,
    cfull,
    outp,
    loc,
    ssem,
    wsem,
    r1,
    r2,
    u1,
    u2,
    gz,
    gy,
    na,
    ns,
    ra,
    rs,
    cz,
    cy,
):
    half = n // 2
    me = lax.axis_index("mem")
    core = lax.axis_index("tp")
    a = me // 2
    b = me % 2
    forks = hidden.shape[0]
    groups = wq.shape[1] // (group_size * HEAD_WIDTH)
    wide = group_size * HEAD_WIDTH
    rows = forks * group_size // n
    lanes = n * rows
    side = half * rows
    mine = b * half + a
    rank_local = up.shape[0]
    pages = kcache.shape[0]
    tokens = kcache.shape[1]
    def send(src, dst, kind, rsem, where):
        copy = pltpu.make_async_remote_copy(
            src_ref=src,
            dst_ref=dst,
            send_sem=ssem.at[kind],
            recv_sem=rsem,
            device_id=where,
            device_id_type=MESH,
        )
        copy.start()

    def take(ref, sem):
        pltpu.make_async_copy(ref, ref, sem).wait()

    def mate():
        return {"mem": me + 1 - 2 * b}

    def far(step):
        return {"mem": 2 * ((a + step) % half) + b}

    order = sorted(range(1, half), key=lambda d: -min(d, half - d))
    spans = sorted(range(1, n), key=lambda o: -min(o, n - o))
    locals_ = []

    def fetch(src, dst):
        copy = pltpu.make_async_copy(src, dst, loc.at[len(locals_)])
        copy.start()
        locals_.append(copy)
        return copy

    dchunks = dbuf.shape[0]
    dwide = dbuf.shape[2]
    get_small = [
        fetch(hidden_in, hidden),
        fetch(adapter_in, adapter),
    ]
    get_down = [fetch(down.at[:, pl.ds(c * dwide, dwide)], dbuf.at[c]) for c in range(dchunks)]
    get_q, get_up = [], []

    def fetch_piece(g):
        columns = pl.ds(g * wide, wide)
        get_q.append(fetch(wq.at[:, columns], wqbuf.at[g]))
        get_up.append(fetch(up.at[:, :, columns], upbuf.at[g]))

    barrier = pltpu.get_barrier_semaphore()
    for o in range(1, n):
        pl.semaphore_signal(barrier, inc=1, device_id={"mem": (me + o) % n}, device_id_type=MESH)
    pl.semaphore_signal(barrier, inc=1, device_id={"tp": 1 - core}, device_id_type=MESH)

    for item in get_small:
        item.wait()
    h = hidden[...]
    ids = adapter[...].astype(F32)
    eye = lax.broadcasted_iota(jnp.int32, (forks, forks), 0) == lax.broadcasted_iota(
        jnp.int32, (forks, forks), 1
    )
    id_column = jnp.sum(jnp.where(eye, ids, 0.0), axis=1, keepdims=True)
    per_tile = 128 // ADAPTER_RANK
    lane_part = (
        lax.broadcasted_iota(jnp.int32, (forks, 128), 1) // ADAPTER_RANK
    ).astype(F32)
    folded = jnp.zeros((forks, 128), F32)
    for c in range(dchunks):
        get_down[c].wait()
        if c == dchunks - 2:
            get_k = fetch(wk, kvbuf.at[0])
            get_v = fetch(wv, kvbuf.at[1])
            fetch_piece(0)
            get_slots = fetch(slots_in, slots)
            get_selection = fetch(selection_in, selection)
        act = dot(h, dbuf[c])
        for t in range(dwide // 128):
            first = (c * (dwide // 128) + t) * per_tile
            folded += jnp.where(
                id_column - float(first) == lane_part, act[:, t * 128 : (t + 1) * 128], 0.0
            )
    for g in range(1, groups):
        fetch_piece(g)
    flipped = jnp.transpose(folded)
    rank_part = flipped[:ADAPTER_RANK]
    for t in range(1, per_tile):
        rank_part += flipped[t * ADAPTER_RANK : (t + 1) * ADAPTER_RANK]
    for j in range(n):
        rtx[j] = rank_part[j * rank_local : (j + 1) * rank_local]
    pl.semaphore_wait(barrier, n)
    for o in spans:
        to = (me + o) % n
        send(rtx.at[to], rrx.at[o - 1], 0, wsem.at[0], {"mem": to})

    def split(g, total):
        for m in range(n):
            first, head = (m // group_size) * rows, (m % group_size) * HEAD_WIDTH
            part[g, m % 2, m // 2] = total[first : first + rows, head : head + HEAD_WIDTH]

    def encode(x):
        unit = jnp.maximum(jnp.max(jnp.abs(x), axis=0, keepdims=True), 1e-30) * (1.0 / 32000.0)
        return jnp.round(x * (1.0 / unit)).astype(jnp.int32).astype(jnp.int16), unit

    def decode(code, unit):
        return code.astype(jnp.int32).astype(F32) * unit

    def reduce_near(g):
        if DIRECT_S[g]:
            for s in range(n):
                code0[g, s], unit0[g, s] = encode(part[g, s // half, s % half])
            tx2[g, a] = part[g, b, a]
            for o in spans:
                to = (me + o) % n
                s = (to % 2) * half + to // 2
                where = {"mem": to}
                send(code0.at[g, s], got2.at[g, o - 1], 14, r2.at[g], where)
                send(unit0.at[g, s], gotu2.at[g, o - 1], 15, u2.at[g], where)
            return
        for s in range(half):
            code1[g, s], unit1[g, s] = encode(part[g, 1 - b, s])
        send(code1.at[g], got1.at[g], 1, r1.at[g], mate())
        send(unit1.at[g], gotu1.at[g], 12, u1.at[g], mate())

    def reduce_far(g):
        if DIRECT_S[g]:
            return
        take(got1.at[g], r1.at[g])
        take(gotu1.at[g], u1.at[g])
        for s in range(half):
            total = part[g, b, s] + decode(got1[g, s], gotu1[g, s])
            tx2[g, s] = total
            code2[g, s], unit2[g, s] = encode(total)
        for d in order:
            s = (a + d) % half
            send(code2.at[g, s], got2.at[g, d - 1], 2, r2.at[g], far(d))
            send(unit2.at[g, s], gotu2.at[g, d - 1], 13, u2.at[g], far(d))

    def reduce_end(g):
        merged = tx2[g, a]
        count = n - 1 if DIRECT_S[g] else half - 1
        take(got2.at[g, pl.ds(0, count)], r2.at[g])
        take(gotu2.at[g, pl.ds(0, count)], u2.at[g])
        for o in range(count):
            merged = merged + decode(got2[g, o], gotu2[g, o])
        qfull[g, mine] = merged.astype(BF16)

    def gather(buf, g, kind, zsem, direct):
        own = buf.at[g, mine]
        if direct:
            for o in spans:
                send(own, own, kind, zsem.at[g], {"mem": (me + o) % n})
        else:
            for d in order:
                send(own, own, kind, zsem.at[g], far(d))

    def forward(buf, g, kind, zsem, ysem, direct):
        if not direct:
            take(buf.at[g, pl.ds(0, half - 1)], zsem.at[g])
            block = buf.at[g, pl.ds(b * half, half)]
            send(block, block, kind, ysem.at[g], mate())

    def arrive(buf, g, zsem, ysem, direct):
        if direct:
            take(buf.at[g, pl.ds(0, n - 1)], zsem.at[g])
        else:
            take(buf.at[g, pl.ds(0, half)], ysem.at[g])

    def share(g):
        reduce_end(g)
        gather(qfull, g, 3, gz, DIRECT_Q[g])

    def pass_on(g):
        forward(qfull, g, 3, gz, gy, DIRECT_Q[g])

    def ready(g):
        arrive(qfull, g, gz, gy, DIRECT_Q[g])

    get_k.wait()
    get_v.wait()
    split(groups, jnp.concatenate([dot(h, kvbuf[0]), dot(h, kvbuf[1])], axis=1))
    reduce_near(groups)
    get_vc = fetch(vcache, vbuf)
    get_kc = fetch(kcache, kbuf)
    get_wo = fetch(wo, wobuf)

    get_slots.wait()
    get_selection.wait()
    lane_id = lax.broadcasted_iota(jnp.int32, (forks, lanes), 1)
    lane_fork = (((lane_id // rows) % half) // (group_size // 2)) * rows + lane_id % rows
    spread_bf = (
        (lane_fork == lax.broadcasted_iota(jnp.int32, (forks, lanes), 0)).astype(F32).astype(BF16)
    )
    slot_ids = me * pages + lax.broadcasted_iota(jnp.int32, (pages, slots.shape[1]), 0)
    match = (slots[...] == slot_ids).astype(F32).astype(BF16)
    chosen = dot(match, selection[...].astype(F32).astype(BF16), ((1,), (1,)))
    selx[...] = dot(chosen.astype(BF16), spread_bf)

    get_q[0].wait()
    base = dot(h, wqbuf[0])
    take(rrx, wsem.at[0])
    ranks = rtx[me]
    for o in range(1, n):
        ranks = ranks + rrx[o - 1]
    ranks = ranks.astype(BF16).astype(F32)
    is_adapter = (
        lax.broadcasted_iota(jnp.int32, (ADAPTER_COUNT, forks), 0) == adapter[...]
    )
    pieces = [jnp.where(is_adapter, ranks[r : r + 1], 0.0) for r in range(rank_local)]
    spread = jnp.transpose(jnp.concatenate(pieces, axis=0)).astype(BF16)

    def produce(g):
        if g:
            get_q[g].wait()
        get_up[g].wait()
        main = dot(h, wqbuf[g]) if g else base
        split(g, main + dot(spread, upbuf[g].reshape(rank_local * ADAPTER_COUNT, wide)))
        reduce_near(g)

    produce(0)
    get_vc.wait()
    vtbuf[:, :, HEAD_WIDTH:, :] = jnp.ones(
        (pages, groups, vtbuf.shape[2] - HEAD_WIDTH, tokens), BF16
    )

    def turn(p, carry):
        for k in range(groups):
            block = vbuf[p, :, k * HEAD_WIDTH : (k + 1) * HEAD_WIDTH]
            vtbuf[p, k, :HEAD_WIDTH, :] = jnp.transpose(block)
        return carry

    batch = math.gcd(pages, BATCH)
    scale = HEAD_WIDTH ** (-0.5)
    scale2 = scale * math.log2(math.e)

    def attend(g):
        columns = pl.ds(g * HEAD_WIDTH, HEAD_WIDTH)
        queries = qfull[g].reshape(lanes, HEAD_WIDTH)
        acc[...] = jnp.zeros_like(acc)
        top0 = jnp.full((1, lanes), neg_floor, F32)
        mass0 = jnp.zeros((1, lanes), F32)

        def block(q, carry):
            top, mass = carry
            first = q * batch
            keys = kbuf[pl.ds(first, batch), :, columns].reshape(batch * tokens, HEAD_WIDTH)
            raw_all = dot(keys, queries, ((1,), (1,)))
            found = []
            new_top = top
            for u in range(batch):
                raw = raw_all[u * tokens : (u + 1) * tokens]
                peak = jnp.max(raw, axis=0, keepdims=True)
                probs = jnp.exp2((raw - peak) * scale2).astype(BF16)
                sums = dot(vtbuf[first + u, g], probs)
                hit = selx[pl.ds(first + u, 1), :] > 0.5
                peak = jnp.where(hit, peak, neg_floor)
                new_top = jnp.maximum(new_top, peak)
                found.append((hit, peak, sums))
            keep = jnp.exp2((top - new_top) * scale2)
            mass = mass * keep
            total = acc[...] * keep
            for hit, peak, sums in found:
                fresh = jnp.where(hit, jnp.exp2((peak - new_top) * scale2), 0.0)
                total = total + sums[:HEAD_WIDTH] * fresh
                mass = mass + sums[HEAD_WIDTH : HEAD_WIDTH + 1] * fresh
            acc[...] = total
            return new_top, mass

        blocks = pages // batch
        return lax.fori_loop(0, blocks, block, (top0, mass0))

    def hand_in(g, top, mass):
        if not DIRECT_R[g]:
            for s in range(2):
                part_lanes = slice(s * side, (s + 1) * side)
                resa[g, s] = acc[:, part_lanes].astype(BF16)
                ress[g, s, 0:1] = top[:, part_lanes]
                ress[g, s, 1:2] = mass[:, part_lanes]
            send(resa.at[g, 1 - b], rxa.at[g], 4, na.at[g], mate())
            send(ress.at[g, 1 - b], rxs.at[g], 5, ns.at[g], mate())
            return
        turned[...] = jnp.transpose(acc[...])
        for s in range(n):
            first = s * rows
            txa[g, s] = turned[first : first + rows].astype(BF16)
            txs[g, s, 0:1] = top[:, first : first + rows]
            txs[g, s, 1:2] = mass[:, first : first + rows]
        for o in spans:
            to = (me + o) % n
            slot = (to % 2) * half + to // 2
            where = {"mem": to}
            send(txa.at[g, slot], fxa.at[g, o - 1], 8, ra.at[g], where)
            send(txs.at[g, slot], fxs.at[g, o - 1], 9, rs.at[g], where)
        owna[g] = turned[pl.ds(pl.multiple_of(mine * rows, rows), rows)]
        owns[g] = txs[g, mine]

    def merge_near(g):
        if DIRECT_R[g]:
            return
        take(rxa.at[g], na.at[g])
        take(rxs.at[g], ns.at[g])
        top_a, top_b = ress[g, b, 0:1], rxs[g, 0:1]
        top = jnp.maximum(top_a, top_b)
        fac_a = jnp.exp2((top_a - top) * scale2)
        fac_b = jnp.exp2((top_b - top) * scale2)
        mass = ress[g, b, 1:2] * fac_a + rxs[g, 1:2] * fac_b
        total = resa[g, b].astype(F32) * fac_a + rxa[g].astype(F32) * fac_b
        turned[:side] = jnp.transpose(total)
        for s in range(half):
            first = s * rows
            txa[g, s] = turned[first : first + rows].astype(BF16)
            txs[g, s, 0:1] = top[:, first : first + rows]
            txs[g, s, 1:2] = mass[:, first : first + rows]
        for d in order:
            slot = (a + d) % half
            send(txa.at[g, slot], fxa.at[g, d - 1], 6, ra.at[g], far(d))
            send(txs.at[g, slot], fxs.at[g, d - 1], 7, rs.at[g], far(d))
        owna[g] = turned[pl.ds(pl.multiple_of(a * rows, rows), rows)]
        owns[g] = txs[g, a]

    def merge(g):
        block = (me // group_size) * (group_size // 2)
        key_new = qfull[groups, (g % 2) * half + block + g // 2].astype(F32)
        at = g + groups
        value_new = qfull[groups, (at % 2) * half + block + at // 2].astype(F32)
        own_score = jnp.sum(qfull[g, mine].astype(F32) * key_new, axis=1, keepdims=True)
        count = n if DIRECT_R[g] else half
        take(fxa.at[g, pl.ds(0, count - 1)], ra.at[g])
        take(fxs.at[g, pl.ds(0, count - 1)], rs.at[g])
        stats = [owns[g, 0:1]] + [fxs[g, o, 0:1] for o in range(count - 1)]
        stats += [owns[g, 1:2]] + [fxs[g, o, 1:2] for o in range(count - 1)]
        columns = jnp.transpose(jnp.concatenate(stats, axis=0))
        tops, masses = columns[:, :count], columns[:, count:]
        top = jnp.maximum(jnp.max(tops, axis=1, keepdims=True), own_score)
        factors = jnp.exp2((tops - top) * scale2)
        own = jnp.exp2((own_score - top) * scale2)
        mass = jnp.sum(masses * factors, axis=1, keepdims=True) + own
        total = owna[g] * factors[:, 0:1] + value_new * own
        for o in range(count - 1):
            total = total + fxa[g, o].astype(F32) * factors[:, o + 1 : o + 2]
        cfull[g, mine] = (total / mass).astype(BF16)
        gather(cfull, g, 10, cz, DIRECT_C[g])

    def pass_context(g):
        forward(cfull, g, 10, cz, cy, DIRECT_C[g])

    wo_ready = []

    def project(g):
        arrive(cfull, g, cz, cy, DIRECT_C[g])
        context = []
        for first in range(0, n, group_size):
            context.append(
                jnp.concatenate(
                    [cfull[g, (m % 2) * half + m // 2] for m in range(first, first + group_size)], axis=1
                )
            )
        context = jnp.concatenate(context, axis=0)
        if not wo_ready:
            get_wo.wait()
            wo_ready.append(True)
        product = dot(context, wobuf[g * wide : (g + 1) * wide, :])
        outp[...] += product


    get_kc.wait()
    outp[...] = jnp.zeros_like(outp)

    def visit(g):
        ready(g)
        hand_in(g, *attend(g))

    steps = {
        "produce": produce,
        "far": reduce_far,
        "turn": lambda g: lax.fori_loop(g * pages // 2, (g + 1) * pages // 2, turn, 0),
        "share": share,
        "pass": pass_on,
        "visit": visit,
        "near": merge_near,
        "ready": ready,
        "merge": merge,
        "context": pass_context,
        "project": project,
    }
    for name, g in order_of(groups):
        steps[name](g)
    keep = fetch(outp, total_a)
    send(outp, total_b, 11, wsem.at[1], {"tp": 1 - core})
    take(total_b, wsem.at[1])
    keep.wait()
    near_r = DIRECT_R.count(False)
    full_r = len(DIRECT_R) - near_r
    full_s = DIRECT_S.count(True)
    near_s = len(DIRECT_S) - full_s
    some, all_s = pl.ds(0, near_s), pl.ds(0, full_s)
    few = pl.ds(0, half - 1)
    sent = [rrx, got1.at[some] if near_s else None, got2.at[some, few] if near_s else None, qfull.at[:, pl.ds(0, n - 1)]]
    if near_r:
        first = pl.ds(0, near_r)
        sent += [rxa.at[first], rxs.at[first]]
        sent += [fxa.at[first, pl.ds(0, half - 1)], fxs.at[first, pl.ds(0, half - 1)]]
    else:
        sent += [None] * 4
    if full_r:
        first = pl.ds(0, full_r)
        sent += [fxa.at[first], fxs.at[first]]
    else:
        sent += [None] * 2
    sent += [cfull.at[:, pl.ds(0, n - 1)], total_b]
    sent += [gotu1.at[some], gotu2.at[some, few]] if near_s else [None] * 2
    sent += [got2.at[all_s], gotu2.at[all_s]] if full_s else [None] * 2
    for kind, ref in enumerate(sent):
        if ref is not None:
            take(ref, ssem.at[kind])


ORDER = (
    ("produce", 1),
    ("turn", 1),
    ("share", 4),
    ("produce", 2),
    ("produce", 3),
    ("far", 1),
    ("share", 0),
    ("far", 2),
    ("share", 1),
    ("far", 3),
    ("turn", 0),
    ("pass", 0),
    ("share", 2),
    ("pass", 1),
    ("visit", 0),
    ("share", 3),
    ("visit", 1),
    ("visit", 2),
    ("pass", 4),
    ("near", 0),
    ("visit", 3),
    ("near", 2),
    ("ready", 4),
    ("merge", 1),
    ("near", 3),
    ("merge", 0),
    ("merge", 2),
    ("context", 1),
    ("merge", 3),
    ("context", 0),
    ("context", 2),
    ("project", 0),
    ("project", 1),
    ("project", 3),
    ("project", 2),
)
DIRECT_Q = (False, False, True, True, False)
DIRECT_S = (True, False, False, False, True)
DIRECT_R = (False, True, False, False)
DIRECT_C = (False, False, False, True)


def order_of(groups):
    if groups == len(DIRECT_R):
        return ORDER
    every = range(groups)
    steps = [("turn", 0), ("turn", 1)] + [("produce", g) for g in range(1, groups)]
    for g in [groups] + list(every):
        steps += [("far", g), ("share", g), ("pass", g)]
    steps += [("ready", groups)]
    for g in every:
        steps += [("visit", g), ("near", g), ("merge", g), ("context", g), ("project", g)]
    return steps


def shards(
    hidden,
    adapter,
    page_cache_slot,
    selection,
    query_projection_weight,
    key_projection_weight,
    value_projection_weight,
    adapter_down_weight,
    adapter_up_weight,
    output_projection_weight,
    prefix_key_cache,
    prefix_value_cache,
):
    n = lax.axis_size("mem")
    half = n // 2
    forks, depth = hidden.shape
    width = query_projection_weight.shape[1]
    kv_width = key_projection_weight.shape[1]
    groups = kv_width // HEAD_WIDTH
    group_size = width // kv_width
    wide = group_size * HEAD_WIDTH
    rows = forks * group_size // n
    lanes = n * rows
    side = half * rows
    out_width = output_projection_weight.shape[1]
    rank_local = adapter_up_weight.shape[0]
    pages, tokens = prefix_key_cache.shape[:2]
    down_width = adapter_down_weight.shape[1]
    chunks = 4
    dma = pltpu.SemaphoreType.DMA
    vmem = pltpu.VMEM
    scratch = [
        vmem((forks, depth), BF16),
        vmem((1, forks), jnp.int32),
        vmem((1, page_cache_slot.shape[0]), jnp.int32),
        vmem(selection.shape, jnp.int32),
        vmem((chunks, depth, down_width // chunks), BF16),
        vmem((2, depth, kv_width), BF16),
        vmem((groups, depth, wide), BF16),
        vmem((groups, rank_local, ADAPTER_COUNT, wide), BF16),
        vmem(prefix_key_cache.shape, BF16),
        vmem(prefix_value_cache.shape, BF16),
        vmem((pages, groups, HEAD_WIDTH + 16, tokens), BF16),
        vmem(output_projection_weight.shape, BF16),
        vmem((n, rank_local, forks), F32),
        vmem((n - 1, rank_local, forks), F32),
        vmem((groups + 1, 2, half, rows, HEAD_WIDTH), F32),
        vmem((groups + 1, half, rows, HEAD_WIDTH), F32),
        vmem((groups + 1, n, rows, HEAD_WIDTH), jnp.int16),
        vmem((groups + 1, n, 1, HEAD_WIDTH), F32),
        vmem((groups + 1, half, rows, HEAD_WIDTH), jnp.int16),
        vmem((groups + 1, half, 1, HEAD_WIDTH), F32),
        vmem((groups + 1, half, rows, HEAD_WIDTH), jnp.int16),
        vmem((groups + 1, half, 1, HEAD_WIDTH), F32),
        vmem((groups + 1, half, rows, HEAD_WIDTH), jnp.int16),
        vmem((groups + 1, half, 1, HEAD_WIDTH), F32),
        vmem((groups + 1, n - 1, rows, HEAD_WIDTH), jnp.int16),
        vmem((groups + 1, n - 1, 1, HEAD_WIDTH), F32),
        vmem((groups + 1, n, rows, HEAD_WIDTH), BF16),
        vmem((pages, lanes), F32),
        vmem((HEAD_WIDTH, lanes), F32),
        vmem((lanes, HEAD_WIDTH), F32),
        vmem((groups, 2, HEAD_WIDTH, side), BF16),
        vmem((groups, 2, 2, side), F32),
        vmem((groups, HEAD_WIDTH, side), BF16),
        vmem((groups, 2, side), F32),
        vmem((groups, n, rows, HEAD_WIDTH), BF16),
        vmem((groups, n, 2, rows), F32),
        vmem((groups, rows, HEAD_WIDTH), F32),
        vmem((groups, 2, rows), F32),
        vmem((groups, n - 1, rows, HEAD_WIDTH), BF16),
        vmem((groups, n - 1, 2, rows), F32),
        vmem((groups, n, rows, HEAD_WIDTH), BF16),
        vmem((forks, out_width), F32),
        dma((chunks + 2 + 2 * groups + 8,)),
        dma((16,)),
        dma((2,)),
        dma((groups + 1,)),
        dma((groups + 1,)),
        dma((groups + 1,)),
        dma((groups + 1,)),
        dma((groups + 1,)),
        dma((groups + 1,)),
        dma((groups,)),
        dma((groups,)),
        dma((groups,)),
        dma((groups,)),
        dma((groups,)),
        dma((groups,)),
    ]
    large = pl.BlockSpec(memory_space=pl.ANY)
    halves = pl.pallas_call(
        functools.partial(kernel, n, group_size),
        out_shape=[jax.ShapeDtypeStruct((forks, out_width), F32)] * 2,
        in_specs=[large] * 12,
        out_specs=[large] * 2,
        scratch_shapes=scratch,
        compiler_params=pltpu.CompilerParams(
            collective_id=0, has_side_effects=True, vmem_limit_bytes=60 * 1024 * 1024
        ),
    )(
        hidden,
        adapter.reshape(1, forks),
        page_cache_slot.reshape(1, page_cache_slot.shape[0]),
        selection,
        query_projection_weight,
        key_projection_weight,
        value_projection_weight,
        adapter_down_weight,
        adapter_up_weight,
        output_projection_weight,
        prefix_key_cache,
        prefix_value_cache,
    )
    return (halves[0] + halves[1]).astype(BF16)


def solution(mesh):
    return jax.shard_map(
        shards,
        mesh=mesh,
        in_specs=(
            P("groups", "mem"),
            P("groups"),
            P("groups"),
            P("groups", None),
            P("mem", "tp"),
            P("mem", "tp"),
            P("mem", "tp"),
            P("mem", None),
            P("mem", None, "tp"),
            P("tp", "mem"),
            P(("groups", "mem"), None, "tp"),
            P(("groups", "mem"), None, "tp"),
        ),
        out_specs=P("groups", "mem"),
        check_vma=False,
    )
```
